128 devices in a mesh: gx: 4 (over z), gy: 4 (over x), gz: 8 (over y, core).
Axes of the slice: x: 4, y: 4, z: 4, core: 2. Of those that a mesh axis runs over, the one named last changes fastest.
Arguments:
- right_side: float32 [64, 64, 128, 256], P('gx', 'gy', 'gz'), may hold values from -35 to 35
- conductivity: float32 [64, 64, 128], P('gx', 'gy', 'gz'), may hold values from 0.25 to 2
- reaction: float32 [64, 64, 128], P('gx', 'gy', 'gz'), may hold values from 0.25 to 4
- leaf_factor: float32 [8, 8, 16, 512, 512], P('gx', 'gy', 'gz'), as said below
- leaf_weight: float32 [8, 8, 16, 512, 64], P('gx', 'gy', 'gz'), may hold values from -0.25 to 0.25
- leaf_skeleton: int32 [8, 8, 16, 64], P('gx', 'gy', 'gz'), may hold values from 0 to 511, as said below
- device_factor: float32 [4, 4, 8, 512, 512], P('gx', 'gy', 'gz'), as said below
- device_weight: float32 [4, 4, 8, 512, 256], P('gx', 'gy', 'gz'), may hold values from -0.25 to 0.25
- device_skeleton: int32 [4, 4, 8, 256], P('gx', 'gy', 'gz'), may hold values from 0 to 511, as said below
- column_factor: float32 [4, 4, 2048, 2048], P('gx', 'gy', 'gz'), as said below
- column_weight: float32 [4, 4, 2048, 128], P('gx', 'gy'), may hold values from -0.125 to 0.125
- column_skeleton: int32 [4, 4, 128], P('gx', 'gy'), may hold values from 0 to 2047, as said below
- top_factor: float32 [2048, 2048], P(('gx', 'gy')), as said below
Outputs:
- solution: float32 [64, 64, 128, 256], P('gx', 'gy', 'gz')
The draws below stay inside these ranges and needn't reach their ends.
Inputs may be any that keep to these rules, and one draw needn't show every extreme that they name: `leaf_factor`: each box's block is symmetric and positive definite. `device_factor`: each domain block's block is symmetric and positive definite. `column_factor`: each column's block is symmetric and positive definite. `top_factor`: symmetric and positive definite. `leaf_skeleton`: the 64 numbers of one box are all different. `device_skeleton`: the 256 numbers of one domain block are all different. `column_skeleton`: the 128 numbers of one column are all different.
All inputs are finite; a program needn't handle non-finite values.
Results may differ from the reference program's by a relative error of at most 0.0001.
Values sent between devices are 32-bit elements; how exact they have to be, the bound alone decides.
A program may use at most 128 MiB of HBM per device.

```python
import math
import jax
import jax.numpy as jnp
from jax import lax

BLOCK = 16
BOX = 8
NRHS = 256
K0 = 64
K1 = 256
K2 = 128
ITERS = 2
LEAF = 512
R1 = 512
R2 = 2048
R_TOP = 2048
NX = 64
NY = 64
NZ = 128
NBX = 8
NBY = 8
NBZ = 16
N_GX = 4
N_GY = 4
N_GZ = 8


def symmetric_dominant(key, shape):
    dimension = shape[-1]
    first, second = jax.random.split(key)
    entries = jax.random.uniform(first, shape, jnp.float32, -0.25, 1.0)
    entries = 0.5 * (entries + jnp.swapaxes(entries, -1, -2))
    diagonal = jax.random.uniform(second, shape[:-1], jnp.float32, 1.2, 2.4)
    identity = jnp.eye(dimension, dtype=jnp.float32)
    return entries / dimension * (1.0 - identity) + identity * diagonal[..., None]


def skeleton_draw(key, leading, choices, count):
    full_shape = leading + (choices,)
    scores = jax.random.randint(key, full_shape, 0, 262144)
    scores = scores * choices + lax.broadcasted_iota(jnp.int32, full_shape, len(leading))
    ranked = jnp.argsort(scores, axis=-1, stable=True)
    return ranked[..., :count].astype(jnp.int32)


def draw_right_side(key, part):
    full_shape = (NX, NY, NZ, NRHS)
    place_x = lax.broadcasted_iota(jnp.float32, full_shape, 0) / max(NX - 1, 1)
    amplitude = 4.0 + 6.0 * place_x
    return jnp.clip(jax.random.normal(key, full_shape, jnp.float32), -3.5, 3.5) * amplitude


def draw_leaf_factor(key, part):
    return symmetric_dominant(jax.random.fold_in(key, 11), (NBX, NBY, NBZ, LEAF, LEAF))


def draw_device_factor(key, part):
    return symmetric_dominant(jax.random.fold_in(key, 12), (N_GX, N_GY, N_GZ, R1, R1))


def draw_column_factor(key, part):
    return symmetric_dominant(jax.random.fold_in(key, 13), (N_GX, N_GY, R2, R2))


def draw_top_factor(key, part):
    return symmetric_dominant(jax.random.fold_in(key, 14), (R_TOP, R_TOP))


def draw_leaf_skeleton(key, part):
    return skeleton_draw(jax.random.fold_in(key, 21), (NBX, NBY, NBZ), LEAF, K0)


def draw_device_skeleton(key, part):
    return skeleton_draw(jax.random.fold_in(key, 22), (N_GX, N_GY, N_GZ), R1, K1)


def draw_column_skeleton(key, part):
    return skeleton_draw(jax.random.fold_in(key, 23), (N_GX, N_GY), R2, K2)


def level_of(rng, extent, shards, smallest, largest):
    loudness, own = 1.0, jax.random.fold_in(rng, 6)
    for dim, parts in shards:
        heights = jnp.exp(jax.random.uniform(jax.random.fold_in(own, dim), (parts,), jnp.float32, smallest / len(shards), largest / len(shards)))
        loudness = loudness * jnp.repeat(heights, extent[dim] // parts).reshape([-1 if axis == dim else 1 for axis in range(len(extent))])
    return loudness


def scatter_about(own_key, dims, width, bound, shards=(), kind=jnp.bfloat16):
    array = width * jax.random.normal(own_key, dims, jnp.float32)
    if shards:
        array = array * level_of(own_key, dims, shards, -0.22, 0.18)
    return jnp.clip(array, -bound, bound).astype(kind)


def setup_inputs(seed: int = 0) -> dict:
    arg_keys = jax.random.split(jax.random.key(seed), 14)
    right_side = draw_right_side(jax.random.fold_in(arg_keys[13], 71), 0)
    conductivity = jnp.clip(jnp.exp(math.log(2.0) - 2.0794415 * jax.random.uniform(arg_keys[1], (NX, NY, NZ), jnp.float32) ** level_of(arg_keys[1], (NX, NY, NZ), ((0, 4), (1, 4), (2, 8)), -0.2, 0.2)), 0.25, 2.0)
    reaction = jnp.clip(jnp.exp(math.log(4.0) - 2.7725887 * jax.random.uniform(arg_keys[2], (NX, NY, NZ), jnp.float32) ** level_of(arg_keys[2], (NX, NY, NZ), ((0, 4), (1, 4), (2, 8)), -0.2, 0.2)), 0.25, 4.0)
    leaf_factor = draw_leaf_factor(jax.random.fold_in(arg_keys[13], 71), 0)
    leaf_weight = scatter_about(arg_keys[4], (NBX, NBY, NBZ, LEAF, K0), LEAF ** -0.5, 0.25, ((0, 4), (1, 4), (2, 8)), jnp.float32)
    leaf_skeleton = draw_leaf_skeleton(jax.random.fold_in(arg_keys[13], 71), 0)
    device_factor = draw_device_factor(jax.random.fold_in(arg_keys[13], 71), 0)
    device_weight = scatter_about(arg_keys[7], (N_GX, N_GY, N_GZ, R1, K1), R1 ** -0.5, 0.25, ((0, 4), (1, 4), (2, 8)), jnp.float32)
    device_skeleton = draw_device_skeleton(jax.random.fold_in(arg_keys[13], 71), 0)
    column_factor = draw_column_factor(jax.random.fold_in(arg_keys[13], 71), 0)
    column_weight = scatter_about(arg_keys[10], (N_GX, N_GY, R2, K2), R2 ** -0.5, 0.125, ((0, 4), (1, 4)), jnp.float32)
    column_skeleton = draw_column_skeleton(jax.random.fold_in(arg_keys[13], 71), 0)
    top_factor = draw_top_factor(jax.random.fold_in(arg_keys[13], 71), 0)
    return dict(right_side=right_side, conductivity=conductivity, reaction=reaction, leaf_factor=leaf_factor, leaf_weight=leaf_weight, leaf_skeleton=leaf_skeleton, device_factor=device_factor, device_weight=device_weight, device_skeleton=device_skeleton, column_factor=column_factor, column_weight=column_weight, column_skeleton=column_skeleton, top_factor=top_factor)


highest = lax.Precision.HIGHEST


def neighbour_slices():
    listing = []
    for axis_number in (0, 1, 2):
        for upper in (True, False):
            picked = [slice(1, -1), slice(1, -1), slice(1, -1)]
            picked[axis_number] = slice(2, None) if upper else slice(0, -2)
            listing.append(tuple(picked))
    return listing


def apply_operator(vector_field, conductivity, reaction):
    padded_cond = jnp.pad(conductivity, 1)
    padded_field = jnp.pad(vector_field, ((1, 1), (1, 1), (1, 1), (0, 0)))
    result = reaction[..., None] * vector_field
    for picked in neighbour_slices():
        coefficient = (0.5 * (conductivity + padded_cond[picked]))[..., None]
        result = result + coefficient * (vector_field - padded_field[picked])
    return result


def pick_rows(values, skeleton):
    leading = skeleton.shape[:-1]
    flat_values = values.reshape((-1,) + values.shape[-2:])
    flat_index = skeleton.reshape((-1, skeleton.shape[-1]))
    chosen = jax.vmap(lambda matrix, rows_index: matrix[rows_index])(flat_values, flat_index)
    return chosen.reshape(leading + chosen.shape[-2:])


def place_rows(values, skeleton, row_count):
    leading = skeleton.shape[:-1]
    flat_values = values.reshape((-1,) + values.shape[-2:])
    flat_index = skeleton.reshape((-1, skeleton.shape[-1]))

    def place_one(matrix, rows_index):
        return jnp.zeros((row_count, matrix.shape[-1]), matrix.dtype).at[rows_index].add(matrix)

    placed = jax.vmap(place_one)(flat_values, flat_index)
    return placed.reshape(leading + placed.shape[-2:])


def restrict(values, skeleton, weight):
    return pick_rows(values, skeleton) + jnp.einsum("...rk,...rn->...kn", weight, values, precision=highest)


def lift(coarse, skeleton, weight, row_count):
    return place_rows(coarse, skeleton, row_count) + jnp.einsum("...rk,...kn->...rn", weight, coarse, precision=highest)


def precondition(residual, leaf_factor, leaf_weight, leaf_skeleton, device_factor, device_weight, device_skeleton, column_factor, column_weight, column_skeleton, top_factor):
    systems = residual.shape[-1]
    per_side = BLOCK // BOX
    leaf_size = BOX * BOX * BOX
    boxes_x = NX // BOX
    boxes_y = NY // BOX
    boxes_z = NZ // BOX
    leaf_values = residual.reshape(boxes_x, BOX, boxes_y, BOX, boxes_z, BOX, systems).transpose(0, 2, 4, 1, 3, 5, 6).reshape(boxes_x, boxes_y, boxes_z, leaf_size, systems)
    leaf_up = restrict(leaf_values, leaf_skeleton, leaf_weight)
    device_values = leaf_up.reshape(N_GX, per_side, N_GY, per_side, N_GZ, per_side, K0, systems).transpose(0, 2, 4, 1, 3, 5, 6, 7).reshape(N_GX, N_GY, N_GZ, R1, systems)
    device_up = restrict(device_values, device_skeleton, device_weight)
    column_values = device_up.reshape(N_GX, N_GY, R2, systems)
    column_up = restrict(column_values, column_skeleton, column_weight)
    top_values = column_up.reshape(R_TOP, systems)
    top_result = jnp.dot(top_factor, top_values, precision=highest)
    column_result = jnp.einsum("abrm,abmn->abrn", column_factor, column_values, precision=highest) + lift(top_result.reshape(N_GX, N_GY, K2, systems), column_skeleton, column_weight, R2)
    device_result = jnp.einsum("abcrm,abcmn->abcrn", device_factor, device_values, precision=highest) + lift(column_result.reshape(N_GX, N_GY, N_GZ, K1, systems), device_skeleton, device_weight, R1)
    leaf_coarse = device_result.reshape(N_GX, N_GY, N_GZ, per_side, per_side, per_side, K0, systems).transpose(0, 3, 1, 4, 2, 5, 6, 7).reshape(boxes_x, boxes_y, boxes_z, K0, systems)
    leaf_result = jnp.einsum("abclm,abcmn->abcln", leaf_factor, leaf_values, precision=highest) + lift(leaf_coarse, leaf_skeleton, leaf_weight, leaf_size)
    return leaf_result.reshape(boxes_x, boxes_y, boxes_z, BOX, BOX, BOX, systems).transpose(0, 3, 1, 4, 2, 5, 6).reshape(NX, NY, NZ, systems)


def reference(right_side, conductivity, reaction, leaf_factor, leaf_weight, leaf_skeleton, device_factor, device_weight, device_skeleton, column_factor, column_weight, column_skeleton, top_factor):
    def smoothing(values):
        return precondition(values, leaf_factor, leaf_weight, leaf_skeleton, device_factor, device_weight, device_skeleton, column_factor, column_weight, column_skeleton, top_factor)

    solution = jnp.zeros_like(right_side)
    residual = right_side
    corrected = smoothing(residual)
    direction = corrected
    energy = jnp.sum(residual * corrected, axis=(0, 1, 2))
    for iteration in range(ITERS):
        applied = apply_operator(direction, conductivity, reaction)
        step_length = energy / jnp.sum(direction * applied, axis=(0, 1, 2))
        solution = solution + step_length * direction
        residual = residual - step_length * applied
        if iteration + 1 < ITERS:
            corrected = smoothing(residual)
            energy_new = jnp.sum(residual * corrected, axis=(0, 1, 2))
            direction = corrected + (energy_new / energy) * direction
            energy = energy_new
    return solution
```

```python
import jax
import jax.numpy as jnp
from jax import lax
from jax.experimental import pallas as pl
from jax.experimental.pallas import tpu as pltpu
from jax.sharding import PartitionSpec as P

F32, BF16 = jnp.float32, jnp.bfloat16
MESH = pl.DeviceIdType.MESH
B = 16
N = 256
NPQ, NS = 16, 8
PIECE = N // NS


def split(value):
    high = value.astype(BF16)
    return high, (value - high.astype(F32)).astype(BF16)


def mm(a, b):
    return jnp.dot(a, b, preferred_element_type=F32)


def mm_nt(a, b):
    return lax.dot_general(a, b, (((1,), (1,)), ((), ())), preferred_element_type=F32)


def dot3(a, b, product=mm):
    a_high, a_low = split(a)
    b_high, b_low = split(b)
    return product(a_high, b_high) + product(a_high, b_low) + product(a_low, b_high)


def each(first, count, body):
    def step(i, carry):
        body(i)
        return carry

    lax.fori_loop(first, count, step, 0)


def box_of(b, lead):
    x, y, z = lax.div(b, 4), lax.rem(lax.div(b, 2), 2), lax.rem(b, 2)
    return (
        pl.ds(8 * x + lead, 8),
        pl.ds(8 * y + lead, 8),
        pl.ds(pl.multiple_of(8 * z, 8), 8),
        slice(None),
    )


def kernel(
    rhs_hbm,
    half_hbm,
    react_hbm,
    leaf_hbm,
    leaf_v_hbm,
    dev_hbm,
    dev_v_hbm,
    col_hbm,
    col_v_hbm,
    top_hbm,
    out_hbm,
    rhs,
    half,
    react,
    leaf,
    leaf_hi,
    leaf_lo,
    leaf_v,
    leaf_vt,
    leaf_v3,
    dev,
    dev_v,
    dev_vt,
    col,
    col_v,
    col_vt,
    top,
    field,
    image,
    dev_in,
    dev_out,
    up_t,
    gath,
    rs,
    ag,
    tg,
    ar1,
    ar2,
    zsend,
    zrecv,
    hzsend,
    hzrecv,
    loc_sem,
    out_sem,
    gath_s,
    gath_r,
    rs_s,
    rs_r,
    ag_s,
    ag_r,
    tg_s,
    tg_r,
    a1_s,
    a1_r,
    a2_s,
    a2_r,
    halo_s,
    halo_r,
    hh_s,
    hh_r,
):
    gx, gy, gz = lax.axis_index("gx"), lax.axis_index("gy"), lax.axis_index("gz")
    pq = gx * 4 + gy
    chip, core = lax.div(gz, 2), lax.rem(gz, 2)
    mate = gz + 1 - 2 * core
    inner = pl.ds(1, B)

    def plane_id(peer):
        return {"gx": lax.div(peer, 4), "gy": lax.rem(peer, 4)}

    def local(i, src, dst):
        return pltpu.make_async_copy(src, dst, loc_sem.at[i])

    loads = [
        local(0, rhs_hbm, rhs),
        local(1, leaf_v_hbm, leaf_v),
        local(2, dev_v_hbm, dev_v),
        local(3, col_v_hbm, col_v),
        local(4, half_hbm, half.at[inner, inner]),
        local(5, dev_hbm, dev),
        local(6, top_hbm, top),
        local(7, col_hbm, col),
        local(8, react_hbm, react),
    ]
    leaf_loads = [local(9 + b, leaf_hbm.at[b], leaf.at[b]) for b in range(8)]
    for copy in loads[:4] + leaf_loads[:2] + loads[4:] + leaf_loads[2:]:
        copy.start()

    barrier = pltpu.get_barrier_semaphore()

    def greet_column(d):
        pl.semaphore_signal(
            barrier, inc=1, device_id={"gz": lax.rem(gz + d, NS)}, device_id_type=MESH
        )

    def greet_plane(d):
        pl.semaphore_signal(
            barrier, inc=1, device_id=plane_id(lax.rem(pq + d, NPQ)), device_id_type=MESH
        )

    each(1, NS, greet_column)
    each(1, NPQ, greet_plane)
    pl.semaphore_wait(barrier, NS - 1 + NPQ - 1)

    def remote(src, dst, send, recv, device):
        return pltpu.make_async_remote_copy(
            src_ref=src,
            dst_ref=dst,
            send_sem=send,
            recv_sem=recv,
            device_id=device,
            device_id_type=MESH,
        )

    def column_start(buf, send, recv, k):
        def body(d):
            peer = lax.rem(gz + d, NS)
            remote(
                buf.at[k, gz], buf.at[k, gz], send.at[k, peer], recv.at[k, gz], {"gz": peer}
            ).start()

        each(1, NS, body)

    def column_wait(buf, send, recv, k):
        def body(d):
            peer = lax.rem(gz + d, NS)
            remote(
                buf.at[k, gz], buf.at[k, peer], send.at[k, peer], recv.at[k, peer], {"gz": peer}
            ).wait()

        each(1, NS, body)

    def plane_start(buf, send, recv, k):
        def body(d):
            peer = lax.rem(pq + d, NPQ)
            remote(
                buf.at[k, pq], buf.at[k, pq], send.at[k, peer], recv.at[k, pq], plane_id(peer)
            ).start()

        each(1, NPQ, body)

    def plane_wait(buf, send, recv, k):
        def body(d):
            peer = lax.rem(pq + d, NPQ)
            remote(
                buf.at[k, pq], buf.at[k, peer], send.at[k, peer], recv.at[k, peer], plane_id(peer)
            ).wait()

        each(1, NPQ, body)

    sides = ((gx, 4, "gx"), (gy, 4, "gy"), (gz, NS, "gz"))

    def layers(array, zs, zr):
        return (
            ((array.at[B, inner], array.at[0, inner]), (array.at[1, inner], array.at[B + 1, inner])),
            ((array.at[inner, B], array.at[inner, 0]), (array.at[inner, 1], array.at[inner, B + 1])),
            ((zs.at[1], zr.at[0]), (zs.at[0], zr.at[1])),
        )

    def halo_copies(array, zs, zr, send, recv):
        copies = []
        for axis, ((place, extent, name), pairs) in enumerate(zip(sides, layers(array, zs, zr))):
            for way, (src, dst) in enumerate(pairs):
                there = place + 1 if way == 0 else place - 1
                exists = place < extent - 1 if way == 0 else place > 0
                arrives = place > 0 if way == 0 else place < extent - 1
                i = 2 * axis + way
                copies.append(
                    (remote(src, dst, send.at[i], recv.at[i], {name: there}), exists, arrives, dst)
                )
        return copies

    def halo_start(copies):
        for copy, exists, _, _ in copies:
            pl.when(exists)(copy.start)

    def halo_zero(copies):
        for _, _, arrives, dst in copies:

            @pl.when(jnp.logical_not(arrives))
            def _():
                dst[...] = jnp.zeros(dst.shape, F32)

    def halo_wait(copies):
        for copy, exists, arrives, _ in copies:
            pl.when(exists)(copy.wait_send)
            pl.when(arrives)(copy.wait_recv)

    def pack_z(array, zs):
        def body(x):
            zs[0, x] = array[x + 1, 1 : B + 1, 0, :]
            zs[1, x] = array[x + 1, 1 : B + 1, B - 1, :]

        each(0, B, body)

    hh = halo_copies(half, hzsend, hzrecv, hh_s, hh_r)
    halos = [
        halo_copies(field.at[k], zsend.at[k], zrecv.at[k], halo_s.at[k], halo_r.at[k])
        for k in range(2)
    ]

    def restrict_all(src, k):
        def leaf_box(b):
            u_high, u_low = split(src[box_of(b, 0)].reshape(512, N))
            both = mm(leaf_vt[b], u_high)
            total = both[:64] + both[64:] + mm(leaf_vt[b, :64], u_low)
            dev_in[pl.ds(pl.multiple_of(b * 64, 64), 64), :] = total

        each(0, 8, leaf_box)
        device_up = dot3(dev_vt[...], dev_in[...])
        gath[k, gz] = device_up
        up_t[k] = dot3(col_vt[...], device_up).T
        rs[k, gz] = up_t[k, pl.ds(pl.multiple_of(gz * PIECE, PIECE), PIECE), :]

    def rs_start(k):
        def body(d):
            peer = lax.rem(gz + d, NS)
            remote(
                up_t.at[k, pl.ds(pl.multiple_of(peer * PIECE, PIECE), PIECE)],
                rs.at[k, gz],
                rs_s.at[k, peer],
                rs_r.at[k, gz],
                {"gz": peer},
            ).start()

        each(1, NS, body)

    def rs_wait(k):
        def body(d):
            peer = lax.rem(gz + d, NS)
            remote(
                up_t.at[k, pl.ds(pl.multiple_of(peer * PIECE, PIECE), PIECE)],
                rs.at[k, peer],
                rs_s.at[k, peer],
                rs_r.at[k, peer],
                {"gz": peer},
            ).wait()

        each(1, NS, body)

    def gath_copies(k):
        direct = [
            remote(gath.at[k, gz], gath.at[k, gz], gath_s.at[k, 0], gath_r.at[k, gz], {"gz": mate})
        ]
        passed, arrivals = [], []
        for i, j in enumerate((1, 3, 2)):
            peer = lax.rem(chip + j, 4) * 2 + core
            direct.append(
                remote(
                    gath.at[k, gz],
                    gath.at[k, gz],
                    gath_s.at[k, 1 + i],
                    gath_r.at[k, gz],
                    {"gz": peer},
                )
            )
            back = lax.rem(chip + j, 4) * 2 + core
            arrivals.append(
                remote(
                    gath.at[k, back],
                    gath.at[k, back],
                    gath_s.at[k, 4 + i],
                    gath_r.at[k, back],
                    {"gz": mate},
                )
            )
            other = lax.rem(chip + j, 4) * 2 + 1 - core
            passed.append(
                remote(
                    gath.at[k, other],
                    gath.at[k, other],
                    gath_s.at[k, 4 + i],
                    gath_r.at[k, other],
                    {"gz": mate},
                )
            )
        from_mate = remote(
            gath.at[k, mate], gath.at[k, mate], gath_s.at[k, 0], gath_r.at[k, mate], {"gz": mate}
        )
        return direct, arrivals, passed, from_mate

    def leaf_products(src, k, first, last):
        def body(b):
            u_high, u_low = split(src[box_of(b, 0)].reshape(512, N))
            if k == 0:
                pltpu.make_async_copy(leaf_hbm.at[b], leaf.at[b], loc_sem.at[9 + b]).wait()
                high, low = split(leaf[b])
                leaf_hi[b] = high
                leaf_lo[b] = low
            else:
                high, low = leaf_hi[b], leaf_lo[b]
            total = mm(high, u_high) + mm(high, u_low) + mm(low, u_high)
            field[(k,) + box_of(b, 1)] = total.reshape(8, 8, 8, N)

        each(first, last, body)

    def precondition(src, k, middle, last_step):
        restrict_all(src, k)
        rs_start(k)
        direct, arrivals, passed, from_mate = gath_copies(k)
        for copy in direct:
            copy.start()
        middle()
        leaf_products(src, k, 0, 3)
        rs_wait(k)
        total = rs[k, 0]
        for i in range(1, NS):
            total = total + rs[k, i]
        ag[k, pq] = total
        plane_start(ag, ag_s, ag_r, k)
        leaf_products(src, k, 3, 6)
        plane_wait(ag, ag_s, ag_r, k)
        if k == 0:
            loads[6].wait()
        tops = jnp.concatenate([ag[k, i] for i in range(NPQ)], axis=1)
        tg[k, gz] = dot3(tops, top[...], mm_nt)
        column_start(tg, tg_s, tg_r, k)
        for copy in arrivals:
            copy.wait_recv()
            copy.start()
        leaf_products(src, k, 6, 8)
        if k == 0:
            loads[5].wait()
            loads[7].wait()
        dev_out[...] = dot3(dev[...], dev_in[...])
        from_mate.wait_recv()
        for copy in passed:
            copy.wait_recv()
        near = dot3(col[...], gath[k].reshape(NS * 256, N))
        column_wait(tg, tg_s, tg_r, k)
        column_out = near + dot3(col_v[...], tg[k].reshape(N, 128), mm_nt)
        dev_out[...] += dot3(dev_v[...], column_out)
        for copy in direct + arrivals:
            copy.wait_send()
        last_step()

    def lift_boxes(k, finish):
        def body(b):
            high, low = split(dev_out[pl.ds(pl.multiple_of(b * 64, 64), 64), :])
            stacked = jnp.concatenate([high, low, high, jnp.zeros_like(high)], axis=0)
            place = (k,) + box_of(b, 1)
            total = field[place].reshape(512, N) + mm(leaf_v3[b], stacked)
            finish(b, place, total.reshape(8, 8, 8, N))

        each(0, 8, body)

    def stencil(k, use):
        rows = lax.broadcasted_iota(jnp.int32, (B, N), 0)
        first, last = rows == 0, rows == B - 1
        first_h, last_h = first[:, :128], last[:, :128]

        def shifted(value, low, high, is_first, is_last):
            up = jnp.where(is_last, high, pltpu.roll(value, B - 1, 0))
            down = jnp.where(is_first, low, pltpu.roll(value, 1, 0))
            return up, down

        def body(x, carry):
            energy, curve = carry
            for y in range(B):
                v = field[k, x + 1, y + 1]
                h = half[x + 1, y + 1]
                v_up, v_down = shifted(
                    v, zrecv[k, 0, x, y : y + 1, :], zrecv[k, 1, x, y : y + 1, :], first, last
                )
                h_up, h_down = shifted(
                    h, hzrecv[0, x, y : y + 1, :], hzrecv[1, x, y : y + 1, :], first_h, last_h
                )
                total = react[x, y]
                pairs = (
                    (half[x, y + 1], field[k, x, y + 1]),
                    (half[x + 2, y + 1], field[k, x + 2, y + 1]),
                    (half[x + 1, y], field[k, x + 1, y]),
                    (half[x + 1, y + 2], field[k, x + 1, y + 2]),
                    (h_up, v_up),
                    (h_down, v_down),
                )
                off = None
                for other, value in pairs:
                    face = h + other
                    total = total + face
                    part = jnp.concatenate([face, face], axis=1) * value
                    off = part if off is None else off + part
                applied = jnp.concatenate([total, total], axis=1) * v - off
                residual = use(x, y, applied)
                energy = energy + residual * v
                curve = curve + v * applied
            return energy, curve

        zero = jnp.zeros((B, N), F32)
        return lax.fori_loop(0, B, body, (zero, zero))

    def ar_first(k, energy, curve):
        row = lax.broadcasted_iota(jnp.int32, (8, N), 0)
        e = jnp.sum(energy, axis=0, keepdims=True)
        c = jnp.sum(curve, axis=0, keepdims=True)
        ar1[k, gz] = jnp.where(row == 0, e, jnp.where(row == 1, c, 0.0))
        column_start(ar1, a1_s, a1_r, k)

    def ar_second(k):
        column_wait(ar1, a1_s, a1_r, k)
        total = ar1[k, 0]
        for i in range(1, NS):
            total = total + ar1[k, i]
        ar2[k, pq] = total
        plane_start(ar2, a2_s, a2_r, k)

    def ar_third(k):
        plane_wait(ar2, a2_s, a2_r, k)
        total = ar2[k, 0]
        for i in range(1, NPQ):
            total = total + ar2[k, i]
        return total[0:1], total[1:2]

    loads[1].wait()

    def prepare(b):
        high, low = split(leaf_v[b])
        leaf_vt[b] = jnp.concatenate([high, low], axis=0)
        high, low = high.astype(F32), low.astype(F32)
        leaf_v3[b] = jnp.concatenate([high, high, low, jnp.zeros_like(low)], axis=0).T.astype(BF16)

    each(0, 8, prepare)
    loads[2].wait()
    dev_vt[...] = dev_v[...].T
    loads[3].wait()
    col_vt[...] = col_v[...].T
    loads[0].wait()

    for copies in [hh] + halos:
        halo_zero(copies)

    def send_halves():
        loads[4].wait()
        pack_z(half, hzsend)
        halo_start(hh)

    precondition(rhs, 0, send_halves, lambda: None)

    def keep(b, place, total):
        field[place] = total

    lift_boxes(0, keep)
    pack_z(field.at[0], zsend.at[0])
    halo_start(halos[0])
    halo_wait(hh)
    loads[8].wait()
    halo_wait(halos[0])

    def use_first(x, y, applied):
        image[x, y] = applied
        return rhs[x, y]

    energy, curve = stencil(0, use_first)
    ar_first(0, energy, curve)

    precondition(image, 1, lambda: None, lambda: None)
    ar_second(0)
    energy0, curve0 = ar_third(0)
    step0 = energy0 / curve0

    def subtract(b, place, total):
        field[place] = field[(0,) + place[1:]] - step0.reshape(1, 1, 1, N) * total

    lift_boxes(1, subtract)
    pack_z(field.at[1], zsend.at[1])
    halo_start(halos[1])
    halo_wait(halos[1])

    def use_second(x, y, applied):
        return rhs[x, y] - step0 * image[x, y]

    energy, curve = stencil(1, use_second)
    ar_first(1, energy, curve)
    ar_second(1)
    energy1, curve1 = ar_third(1)
    mixing = energy1 / energy0
    step1 = energy1 / (curve1 - mixing * energy1 / step0)
    ahead = (step0 + step1 * mixing).reshape(1, 1, N)
    last = step1.reshape(1, 1, N)

    def write(x):
        image[x] = ahead * field[0, x + 1, 1 : B + 1] + last * field[1, x + 1, 1 : B + 1]
        pltpu.make_async_copy(image.at[x], out_hbm.at[x], out_sem.at[x]).start()

    each(0, B, write)

    def written(x):
        pltpu.make_async_copy(image.at[x], out_hbm.at[x], out_sem.at[x]).wait()

    each(0, B, written)


def local(
    right_side,
    conductivity,
    reaction,
    leaf_factor,
    leaf_weight,
    leaf_skeleton,
    device_factor,
    device_weight,
    device_skeleton,
    column_factor,
    column_weight,
    column_skeleton,
    top_factor,
):
    def onehot(skeleton, rows, first=0):
        numbers = lax.broadcasted_iota(jnp.int32, (rows, 1), 0) + first
        return (numbers == skeleton[None, :]).astype(F32)

    wide = (B, B, B, 128)
    half = jnp.broadcast_to((0.5 * conductivity)[..., None], wide)
    react = jnp.broadcast_to(reaction[..., None], wide)
    skeleton = leaf_skeleton.reshape(8, 64)
    leaf_v = jnp.swapaxes(leaf_weight.reshape(8, 512, 64), 1, 2) + (
        skeleton[..., None] == lax.broadcasted_iota(jnp.int32, (1, 1, 512), 2)
    ).astype(F32)
    dev_v = device_weight[0, 0, 0] + onehot(device_skeleton[0, 0, 0], 512)
    start = lax.axis_index("gz") * 256
    col_v = lax.dynamic_slice_in_dim(column_weight[0, 0], start, 256, 0) + onehot(
        column_skeleton[0, 0], 256, start
    )
    any_space = pl.BlockSpec(memory_space=pl.ANY)
    dma = pltpu.SemaphoreType.DMA
    vm = pltpu.VMEM
    scratch = [
        vm((B, B, B, N), F32),
        vm((B + 2, B + 2, B, 128), F32),
        vm((B, B, B, 128), F32),
        vm((8, 512, 512), F32),
        vm((8, 512, 512), BF16),
        vm((8, 512, 512), BF16),
        vm((8, 64, 512), F32),
        vm((8, 128, 512), BF16),
        vm((8, 512, 256), BF16),
        vm((512, 512), F32),
        vm((512, 256), F32),
        vm((256, 512), F32),
        vm((256, 2048), F32),
        vm((256, 128), F32),
        vm((128, 256), F32),
        vm((128, 2048), F32),
        vm((2, B + 2, B + 2, B, N), F32),
        vm((B, B, B, N), F32),
        vm((512, N), F32),
        vm((512, N), F32),
        vm((2, N, 128), F32),
        vm((2, NS, 256, N), F32),
        vm((2, NS, PIECE, 128), F32),
        vm((2, NPQ, PIECE, 128), F32),
        vm((2, NS, PIECE, 128), F32),
        vm((2, NS, 8, N), F32),
        vm((2, NPQ, 8, N), F32),
        vm((2, 2, B, B, N), F32),
        vm((2, 2, B, B, N), F32),
        vm((2, B, B, 128), F32),
        vm((2, B, B, 128), F32),
        dma((17,)),
        dma((B,)),
        dma((2, NS)),
        dma((2, NS)),
        dma((2, NS)),
        dma((2, NS)),
        dma((2, NPQ)),
        dma((2, NPQ)),
        dma((2, NS)),
        dma((2, NS)),
        dma((2, NS)),
        dma((2, NS)),
        dma((2, NPQ)),
        dma((2, NPQ)),
        dma((2, 6)),
        dma((2, 6)),
        dma((6,)),
        dma((6,)),
    ]
    return pl.pallas_call(
        kernel,
        out_shape=jax.ShapeDtypeStruct((B, B, B, N), F32),
        in_specs=[any_space] * 10,
        out_specs=any_space,
        scratch_shapes=scratch,
        compiler_params=pltpu.CompilerParams(
            collective_id=0, has_side_effects=True, vmem_limit_bytes=67043328
        ),
        name="cg",
    )(
        right_side,
        half,
        react,
        leaf_factor.reshape(8, 512, 512),
        leaf_v,
        device_factor[0, 0, 0],
        dev_v,
        column_factor[0, 0],
        col_v,
        top_factor,
    )


def solution(mesh):
    cells = P("gx", "gy", "gz")
    in_specs = (cells,) * 10 + (P("gx", "gy"), P("gx", "gy"), P(("gx", "gy"), None))
    return jax.shard_map(local, mesh=mesh, in_specs=in_specs, out_specs=cells, check_vma=False)
```

```python
import jax
import jax.numpy as jnp
from jax import lax
from jax.experimental import pallas as pl
from jax.experimental.pallas import tpu as pltpu
from jax.sharding import PartitionSpec as P

F32, BF16 = jnp.float32, jnp.bfloat16
MESH = pl.DeviceIdType.MESH
B = 16
N = 256
NPQ, NS = 16, 8
PIECE = N // NS


def split(value):
    high = value.astype(BF16)
    return high, (value - high.astype(F32)).astype(BF16)


def mm(a, b):
    return jnp.dot(a, b, preferred_element_type=F32)


def mm_nt(a, b):
    return lax.dot_general(a, b, (((1,), (1,)), ((), ())), preferred_element_type=F32)


def dot3(a, b, product=mm):
    a_high, a_low = split(a)
    b_high, b_low = split(b)
    return product(a_high, b_high) + product(a_high, b_low) + product(a_low, b_high)


def each(first, count, body):
    def step(i, carry):
        body(i)
        return carry

    lax.fori_loop(first, count, step, 0)


def box_of(b, lead):
    x, y, z = lax.div(b, 4), lax.rem(lax.div(b, 2), 2), lax.rem(b, 2)
    return (
        pl.ds(8 * x + lead, 8),
        pl.ds(8 * y + lead, 8),
        pl.ds(pl.multiple_of(8 * z, 8), 8),
        slice(None),
    )


def kernel(
    rhs_hbm,
    cond_hbm,
    react_hbm,
    leaf_hbm,
    leaf_w_hbm,
    leaf_s_hbm,
    dev_hbm,
    dev_w_hbm,
    dev_s_hbm,
    col_hbm,
    col_w_hbm,
    col_s_hbm,
    top_hbm,
    out_hbm,
    rhs,
    cond_raw,
    react_raw,
    leaf_s,
    dev_s,
    col_s,
    half,
    react,
    leaf,
    leaf_hi,
    leaf_lo,
    leaf_v,
    leaf_vt,
    leaf_v3,
    dev,
    dev_v,
    dev_vt,
    col,
    col_v,
    col_vt,
    top,
    field,
    image,
    dev_in,
    dev_out,
    up_t,
    gath,
    near,
    rs,
    ag,
    tg,
    ar1,
    ar2,
    zsend,
    zrecv,
    hzsend,
    hzrecv,
    loc_sem,
    out_sem,
    gath_s,
    gath_r,
    rs_s,
    rs_r,
    ag_s,
    ag_r,
    tg_s,
    tg_r,
    a1_s,
    a1_r,
    a2_s,
    a2_r,
    halo_s,
    halo_r,
    hh_s,
    hh_r,
):
    gx, gy, gz = lax.axis_index("gx"), lax.axis_index("gy"), lax.axis_index("gz")
    pq = gx * 4 + gy
    chip, core = lax.div(gz, 2), lax.rem(gz, 2)
    mate = gz + 1 - 2 * core
    inner = pl.ds(1, B)

    def plane_id(peer):
        return {"gx": lax.div(peer, 4), "gy": lax.rem(peer, 4)}

    def local(i, src, dst):
        return pltpu.make_async_copy(src, dst, loc_sem.at[i])

    loads = [
        local(0, rhs_hbm, rhs),
        local(1, leaf_w_hbm, leaf_v),
        local(2, dev_w_hbm, dev_v),
        local(3, col_w_hbm.at[pl.ds(pl.multiple_of(gz * 256, 256), 256)], col_v),
        local(4, cond_hbm, cond_raw),
        local(5, dev_hbm, dev),
        local(6, top_hbm, top),
        local(7, col_hbm, col),
        local(8, react_hbm, react_raw),
        local(17, leaf_s_hbm, leaf_s),
        local(18, dev_s_hbm, dev_s),
        local(19, col_s_hbm, col_s),
    ]
    leaf_loads = [local(9 + b, leaf_hbm.at[b], leaf.at[b]) for b in range(4)]
    for copy in loads[9:] + loads[1:4] + loads[:1] + leaf_loads[:2] + loads[4:9] + leaf_loads[2:]:
        copy.start()

    barrier = pltpu.get_barrier_semaphore()

    def greet_column(d):
        pl.semaphore_signal(
            barrier, inc=1, device_id={"gz": lax.rem(gz + d, NS)}, device_id_type=MESH
        )

    def greet_plane(d):
        pl.semaphore_signal(
            barrier, inc=1, device_id=plane_id(lax.rem(pq + d, NPQ)), device_id_type=MESH
        )

    each(1, NS, greet_column)
    each(1, NPQ, greet_plane)
    def remote(src, dst, send, recv, device):
        return pltpu.make_async_remote_copy(
            src_ref=src,
            dst_ref=dst,
            send_sem=send,
            recv_sem=recv,
            device_id=device,
            device_id_type=MESH,
        )

    def column_start(buf, send, recv, k):
        def body(d):
            peer = lax.rem(gz + d, NS)
            remote(
                buf.at[k, gz], buf.at[k, gz], send.at[k, peer], recv.at[k, gz], {"gz": peer}
            ).start()

        each(1, NS, body)

    def column_wait(buf, send, recv, k):
        def body(d):
            peer = lax.rem(gz + d, NS)
            remote(
                buf.at[k, gz], buf.at[k, peer], send.at[k, peer], recv.at[k, peer], {"gz": peer}
            ).wait()

        each(1, NS, body)

    def plane_start(buf, send, recv, k):
        def body(d):
            peer = lax.rem(pq + d, NPQ)
            remote(
                buf.at[k, pq], buf.at[k, pq], send.at[k, peer], recv.at[k, pq], plane_id(peer)
            ).start()

        each(1, NPQ, body)

    def plane_wait(buf, send, recv, k):
        def body(d):
            peer = lax.rem(pq + d, NPQ)
            remote(
                buf.at[k, pq], buf.at[k, peer], send.at[k, peer], recv.at[k, peer], plane_id(peer)
            ).wait()

        each(1, NPQ, body)

    sides = ((gx, 4, "gx"), (gy, 4, "gy"), (gz, NS, "gz"))

    def layers(array, zs, zr, halved):
        size = B // 2 if halved else B
        lower, upper = pl.ds(1, size), pl.ds(1 + B - size, size)
        z_lower, z_upper = pl.ds(0, size), pl.ds(B - size, size)
        return (
            ((array.at[B, lower], array.at[0, lower]), (array.at[1, upper], array.at[B + 1, upper])),
            ((array.at[lower, B], array.at[lower, 0]), (array.at[upper, 1], array.at[upper, B + 1])),
            ((zs.at[1, z_lower], zr.at[0, z_lower]), (zs.at[0, z_upper], zr.at[1, z_upper])),
        )

    def halo_copies(array, zs, zr, send, recv, halved=False):
        copies = []
        parts = layers(array, zs, zr, halved)
        for axis, ((place, extent, name), pairs) in enumerate(zip(sides, parts)):
            for way, (src, dst) in enumerate(pairs):
                there = place + 1 if way == 0 else place - 1
                exists = place < extent - 1 if way == 0 else place > 0
                arrives = place > 0 if way == 0 else place < extent - 1
                i = 2 * axis + way
                copies.append(
                    (remote(src, dst, send.at[i], recv.at[i], {name: there}), exists, arrives, dst)
                )
        return copies

    def halo_start(copies):
        for copy, exists, _, _ in copies:
            pl.when(exists)(copy.start)

    def halo_zero(copies):
        for _, _, arrives, dst in copies:

            @pl.when(jnp.logical_not(arrives))
            def _():
                dst[...] = jnp.zeros(dst.shape, F32)

    def halo_wait(copies):
        for copy, exists, arrives, _ in copies:
            pl.when(exists)(copy.wait_send)
            pl.when(arrives)(copy.wait_recv)

    def pack_z(array, zs):
        def body(x):
            zs[0, x] = array[x + 1, 1 : B + 1, 0, :]
            zs[1, x] = array[x + 1, 1 : B + 1, B - 1, :]

        each(0, B, body)

    hh = halo_copies(half, hzsend, hzrecv, hh_s, hh_r)
    halos = [
        halo_copies(field.at[k], zsend.at[k], zrecv.at[k], halo_s.at[k], halo_r.at[k], k == 1)
        for k in range(2)
    ]

    def restrict_all(src, k):
        def leaf_box(b):
            u_high, u_low = split(src[box_of(b, 0)].reshape(512, N))
            both = mm(leaf_vt[b], u_high)
            total = both[:64] + both[64:] + mm(leaf_vt[b, :64], u_low)
            dev_in[pl.ds(pl.multiple_of(b * 64, 64), 64), :] = total

        each(0, 8, leaf_box)
        device_up = dot3(dev_vt[...], dev_in[...])
        gath[k, gz] = device_up
        up_t[k] = dot3(col_vt[...], device_up).T
        rs[k, gz] = up_t[k, pl.ds(pl.multiple_of(gz * PIECE, PIECE), PIECE), :]

    def rs_start(k):
        def body(d):
            peer = lax.rem(gz + d, NS)
            remote(
                up_t.at[k, pl.ds(pl.multiple_of(peer * PIECE, PIECE), PIECE)],
                rs.at[k, gz],
                rs_s.at[k, peer],
                rs_r.at[k, gz],
                {"gz": peer},
            ).start()

        each(1, NS, body)

    def rs_wait(k):
        def body(d):
            peer = lax.rem(gz + d, NS)
            remote(
                up_t.at[k, pl.ds(pl.multiple_of(peer * PIECE, PIECE), PIECE)],
                rs.at[k, peer],
                rs_s.at[k, peer],
                rs_r.at[k, peer],
                {"gz": peer},
            ).wait()

        each(1, NS, body)

    plus, minus, far = [lax.rem(chip + j, 4) * 2 + core for j in (1, 3, 2)]

    def half_block(k, slot, part, sem, to):
        ref = gath.at[k, slot, pl.ds(part * 128, 128)]
        return remote(ref, ref, gath_s.at[k, sem], gath_r.at[k, slot, part], {"gz": to})

    def gath_own(k):
        return [
            half_block(k, gz, part, sem, to)
            for sem, (part, to) in enumerate(
                ((0, plus), (1, minus), (1, plus), (0, minus), (0, mate), (1, mate))
            )
        ]

    def gath_onward(k):
        return [
            half_block(k, slot, part, 6 + sem, to)
            for sem, (slot, part, to) in enumerate(
                (
                    (minus, 0, plus),
                    (plus, 1, minus),
                    (minus, 0, mate),
                    (plus, 1, mate),
                    (minus, 1, mate),
                    (plus, 0, mate),
                    (far, 0, mate),
                    (far, 1, mate),
                )
            )
        ]

    def gath_wait(k, slot):
        for part in range(2):
            half_block(k, slot, part, 0, mate).wait_recv()

    def near_block(k, slot, first=False):
        columns = pl.ds(pl.multiple_of(slot * 256, 256), 256)
        value = dot3(col[:, columns], gath[k, slot])
        near[...] = value if first else near[...] + value

    def leaf_products(src, k, first, last):
        def body(b):
            u_high, u_low = split(src[box_of(b, 0)].reshape(512, N))
            if k == 0:
                slot = lax.rem(b, 4)
                pltpu.make_async_copy(leaf_hbm.at[b], leaf.at[slot], loc_sem.at[9 + b]).wait()
                high, low = split(leaf[slot])
                leaf_hi[b] = high
                leaf_lo[b] = low

                @pl.when(b < 4)
                def _():
                    pltpu.make_async_copy(
                        leaf_hbm.at[b + 4], leaf.at[slot], loc_sem.at[13 + b]
                    ).start()

            else:
                high, low = leaf_hi[b], leaf_lo[b]
            total = mm(high, u_high) + mm(high, u_low) + mm(low, u_high)
            field[(k,) + box_of(b, 1)] = total.reshape(8, 8, 8, N)

        each(first, last, body)

    def precondition(src, k, middle, later):
        restrict_all(src, k)
        if k == 0:
            pl.semaphore_wait(barrier, NS - 1 + NPQ - 1)
        rs_start(k)
        own, onward = gath_own(k), gath_onward(k)
        for copy in own:
            copy.start()
        middle()
        leaf_products(src, k, 0, 3)
        rs_wait(k)
        total = rs[k, 0]
        for i in range(1, NS):
            total = total + rs[k, i]
        ag[k, pq] = total
        plane_start(ag, ag_s, ag_r, k)
        leaf_products(src, k, 3, 5)
        for i in (0, 1):
            onward[2 + i].wait_recv()
            onward[i].start()
            onward[2 + i].start()
        if k == 0:
            loads[6].wait()
        leaf_products(src, k, 5, 6)
        plane_wait(ag, ag_s, ag_r, k)
        tops = jnp.concatenate([ag[k, i] for i in range(NPQ)], axis=1)
        tg[k, gz] = dot3(tops, top[...], mm_nt)
        column_start(tg, tg_s, tg_r, k)
        for i in (4, 5):
            onward[i].wait_recv()
            onward[i].start()
        leaf_products(src, k, 6, 8)
        for i in (6, 7):
            onward[i].wait_recv()
            onward[i].start()
        if k == 0:
            loads[5].wait()
            loads[7].wait()
        dev_out[...] = dot3(dev[...], dev_in[...])
        later()
        near_block(k, gz, True)
        for slot in (minus, plus, far):
            near_block(k, slot)
        for base in (gz, minus, plus, far):
            slot = base + mate - gz
            gath_wait(k, slot)
            near_block(k, slot)
        column_wait(tg, tg_s, tg_r, k)
        column_out = near[...] + dot3(col_v[...], tg[k].reshape(N, 128), mm_nt)
        dev_out[...] += dot3(dev_v[...], column_out)
        for copy in own + onward:
            copy.wait_send()

    def lift_boxes(k, finish):
        def body(b):
            high, low = split(dev_out[pl.ds(pl.multiple_of(b * 64, 64), 64), :])
            stacked = jnp.concatenate([high, low, high, jnp.zeros_like(high)], axis=0)
            place = (k,) + box_of(b, 1)
            total = field[place].reshape(512, N) + mm(leaf_v3[b], stacked)
            finish(b, place, total.reshape(8, 8, 8, N))

        each(0, 8, body)

    def twice(value):
        return jnp.concatenate([value, value], axis=1)

    def stencil(k, use):
        rows = lax.broadcasted_iota(jnp.int32, (B, 128), 0)
        first, last = rows == 0, rows == B - 1

        def body(x, carry):
            energy, curve = carry
            has_low = jnp.where(x > 0, 1.0, 0.0).astype(F32)
            has_high = jnp.where(x < B - 1, 1.0, 0.0).astype(F32)
            x_low, x_high = jnp.maximum(x, 1), jnp.minimum(x + 2, B)
            for y in range(B):
                v = field[k, x + 1, y + 1]
                h = half[x + 1, y + 1]
                if k == 1:
                    face_up = jnp.where(last, 0.0, h + pltpu.roll(h, B - 1, 0))
                    face_xh = (h + half[x + 2, y + 1]) * has_high
                    applied = (
                        twice(0.5 * react[x, y]) * v
                        - twice(face_xh) * field[k, x_high, y + 1]
                        - twice(face_up) * pltpu.roll(v, B - 1, 0)
                    )
                    if y < B - 1:
                        face_yh = h + half[x + 1, y + 2]
                        applied = applied - twice(face_yh) * field[k, x + 1, y + 2]
                    energy = energy + use(x, y, None) * v
                    curve = curve + v * applied
                    continue
                low, high = hzrecv[0, x, y : y + 1, :], hzrecv[1, x, y : y + 1, :]
                face_up = h + jnp.where(last, high, pltpu.roll(h, B - 1, 0))
                face_down = h + jnp.where(first, low, pltpu.roll(h, 1, 0))
                face_xl, face_xh = h + half[x, y + 1], h + half[x + 2, y + 1]
                face_yl = h + half[x + 1, y] if y == 0 else face_yh
                face_yh = h + half[x + 1, y + 2]
                total = react[x, y] + face_up + face_down + face_xl + face_xh + face_yl + face_yh
                react[x, y] = total
                applied = (
                    twice(total) * v
                    - twice(face_xl * has_low) * field[k, x_low, y + 1]
                    - twice(face_xh * has_high) * field[k, x_high, y + 1]
                    - twice(jnp.where(last, 0.0, face_up)) * pltpu.roll(v, B - 1, 0)
                    - twice(jnp.where(first, 0.0, face_down)) * pltpu.roll(v, 1, 0)
                )
                if y > 0:
                    applied = applied - twice(face_yl) * field[k, x + 1, y]
                if y < B - 1:
                    applied = applied - twice(face_yh) * field[k, x + 1, y + 2]
                energy = energy + use(x, y, applied) * v
                curve = curve + v * applied
            return energy, curve

        zero = jnp.zeros((B, N), F32)
        return lax.fori_loop(0, B, body, (zero, zero))

    def outer_terms(k, curve):
        def body(i, total):
            for side in range(2):
                at = i + B // 2 * side if k == 1 else i
                edge, beyond = (1, 0) if side == 0 else (B, B + 1)
                part = twice(half[edge, at + 1] + half[beyond, at + 1]) * field[k, beyond, at + 1]
                total = total + part * field[k, edge, at + 1]
                if k == 0:
                    image[edge - 1, at] -= part
                part = twice(half[at + 1, edge] + half[at + 1, beyond]) * field[k, at + 1, beyond]
                total = total + part * field[k, at + 1, edge]
                if k == 0:
                    image[at, edge - 1] -= part
                part = twice(hzsend[side, at] + hzrecv[side, at]) * zrecv[k, side, at]
                total = total + part * zsend[k, side, at]
                if k == 0:
                    image[at, :, edge - 1, :] -= part
            return total

        count = B // 2 if k == 1 else B
        total = lax.fori_loop(0, count, body, jnp.zeros((B, N), F32))
        return 2.0 * (curve - total) if k == 1 else curve - total

    def ar_first(k, energy, curve):
        row = lax.broadcasted_iota(jnp.int32, (8, 128), 0)
        e = jnp.sum(energy, axis=0, keepdims=True)
        c = jnp.sum(curve, axis=0, keepdims=True)
        packed = jnp.where(row == 3, c[:, 128:], 0.0)
        for i, line in enumerate((e[:, :128], e[:, 128:], c[:, :128])):
            packed = jnp.where(row == i, line, packed)
        ar1[k, gz] = packed
        column_start(ar1, a1_s, a1_r, k)

    def ar_second(k):
        column_wait(ar1, a1_s, a1_r, k)
        total = ar1[k, 0]
        for i in range(1, NS):
            total = total + ar1[k, i]
        ar2[k, pq] = total
        plane_start(ar2, a2_s, a2_r, k)

    def ar_third(k):
        plane_wait(ar2, a2_s, a2_r, k)
        total = ar2[k, 0]
        for i in range(1, NPQ):
            total = total + ar2[k, i]
        lines = [total[i : i + 1] for i in range(4)]
        return jnp.concatenate(lines[:2], axis=1), jnp.concatenate(lines[2:], axis=1)

    for i in (1, 9, 10, 11):
        loads[i].wait()
    padded = jnp.concatenate([leaf_s[...], jnp.zeros((8, 64), jnp.int32)], axis=1).astype(F32)
    numbers = padded.T[:64]
    chosen_box = lax.broadcasted_iota(jnp.int32, (64, 8), 1)
    places = lax.broadcasted_iota(jnp.int32, (64, 512), 1).astype(F32)

    def prepare(b):
        mine = jnp.sum(jnp.where(chosen_box == b, numbers, 0.0), axis=1, keepdims=True)
        high, low = split(leaf_v[b] + jnp.where(places == mine, 1.0, 0.0))
        leaf_vt[b] = jnp.concatenate([high, low], axis=0)
        high, low = high.astype(F32), low.astype(F32)
        leaf_v3[b] = jnp.concatenate([high, high, low, jnp.zeros_like(low)], axis=0).T.astype(BF16)

    each(0, 8, prepare)
    loads[2].wait()
    rows = lax.broadcasted_iota(jnp.int32, (512, 256), 0)
    dev_v[...] += jnp.where(rows == dev_s[...], 1.0, 0.0)
    dev_vt[...] = dev_v[...].T
    loads[3].wait()
    rows = lax.broadcasted_iota(jnp.int32, (256, 128), 0) + gz * 256
    col_v[...] += jnp.where(rows == col_s[...], 1.0, 0.0)
    col_vt[...] = col_v[...].T
    loads[0].wait()

    for copies in [hh] + halos:
        halo_zero(copies)

    def send_halves():
        loads[4].wait()
        loads[8].wait()
        diagonal = lax.broadcasted_iota(jnp.int32, (B, B), 0) == lax.broadcasted_iota(
            jnp.int32, (B, B), 1
        )

        def spread(line):
            value = jnp.sum(jnp.where(diagonal, line, 0.0), axis=1, keepdims=True)
            return jnp.broadcast_to(value, (B, 128))

        def body(x):
            for y in range(B):
                half[x + 1, y + 1] = 0.5 * spread(cond_raw[x, y : y + 1, :])
                react[x, y] = spread(react_raw[x, y : y + 1, :])

        each(0, B, body)
        pack_z(half, hzsend)
        halo_start(hh)

    precondition(rhs, 0, send_halves, lambda: None)

    def keep(b, place, total):
        field[place] = total

    lift_boxes(0, keep)
    pack_z(field.at[0], zsend.at[0])
    halo_start(halos[0])
    halo_wait(hh)

    def use_first(x, y, applied):
        image[x, y] = applied
        return rhs[x, y]

    energy, curve = stencil(0, use_first)
    halo_wait(halos[0])
    curve = outer_terms(0, curve)
    ar_first(0, energy, curve)

    precondition(image, 1, lambda: ar_second(0), lambda: None)
    energy0, curve0 = ar_third(0)
    step0 = energy0 / curve0

    def subtract(b, place, total):
        field[place] = field[(0,) + place[1:]] - step0.reshape(1, 1, 1, N) * total

    lift_boxes(1, subtract)
    pack_z(field.at[1], zsend.at[1])
    halo_start(halos[1])

    def use_second(x, y, applied):
        return rhs[x, y] - step0 * image[x, y]

    energy, curve = stencil(1, use_second)
    halo_wait(halos[1])
    curve = outer_terms(1, curve)
    ar_first(1, energy, curve)
    ar_second(1)
    energy1, curve1 = ar_third(1)
    mixing = energy1 / energy0
    step1 = energy1 / (curve1 - mixing * energy1 / step0)
    ahead = (step0 + step1 * mixing).reshape(1, 1, N)
    last = step1.reshape(1, 1, N)

    def write(x):
        image[x] = ahead * field[0, x + 1, 1 : B + 1] + last * field[1, x + 1, 1 : B + 1]
        pltpu.make_async_copy(image.at[x], out_hbm.at[x], out_sem.at[x]).start()

    each(0, B, write)

    def written(x):
        pltpu.make_async_copy(image.at[x], out_hbm.at[x], out_sem.at[x]).wait()

    each(0, B, written)


def local(
    right_side,
    conductivity,
    reaction,
    leaf_factor,
    leaf_weight,
    leaf_skeleton,
    device_factor,
    device_weight,
    device_skeleton,
    column_factor,
    column_weight,
    column_skeleton,
    top_factor,
):
    leaf_w = jnp.swapaxes(leaf_weight.reshape(8, 512, 64), 1, 2)
    any_space = pl.BlockSpec(memory_space=pl.ANY)
    dma = pltpu.SemaphoreType.DMA
    vm = pltpu.VMEM
    scratch = [
        vm((B, B, B, N), F32),
        vm((B, B, B), F32),
        vm((B, B, B), F32),
        vm((8, 64), jnp.int32),
        vm((1, 256), jnp.int32),
        vm((1, 128), jnp.int32),
        vm((B + 2, B + 2, B, 128), F32),
        vm((B, B, B, 128), F32),
        vm((4, 512, 512), F32),
        vm((8, 512, 512), BF16),
        vm((8, 512, 512), BF16),
        vm((8, 64, 512), F32),
        vm((8, 128, 512), BF16),
        vm((8, 512, 256), BF16),
        vm((512, 512), F32),
        vm((512, 256), F32),
        vm((256, 512), F32),
        vm((256, 2048), F32),
        vm((256, 128), F32),
        vm((128, 256), F32),
        vm((128, 2048), F32),
        vm((2, B + 2, B + 2, B, N), F32),
        vm((B, B, B, N), F32),
        vm((512, N), F32),
        vm((512, N), F32),
        vm((2, N, 128), F32),
        vm((2, NS, 256, N), F32),
        vm((256, N), F32),
        vm((2, NS, PIECE, 128), F32),
        vm((2, NPQ, PIECE, 128), F32),
        vm((2, NS, PIECE, 128), F32),
        vm((2, NS, 8, 128), F32),
        vm((2, NPQ, 8, 128), F32),
        vm((2, 2, B, B, N), F32),
        vm((2, 2, B, B, N), F32),
        vm((2, B, B, 128), F32),
        vm((2, B, B, 128), F32),
        dma((20,)),
        dma((B,)),
        dma((2, 14)),
        dma((2, NS, 2)),
        dma((2, NS)),
        dma((2, NS)),
        dma((2, NPQ)),
        dma((2, NPQ)),
        dma((2, NS)),
        dma((2, NS)),
        dma((2, NS)),
        dma((2, NS)),
        dma((2, NPQ)),
        dma((2, NPQ)),
        dma((2, 6)),
        dma((2, 6)),
        dma((6,)),
        dma((6,)),
    ]
    return pl.pallas_call(
        kernel,
        out_shape=jax.ShapeDtypeStruct((B, B, B, N), F32),
        in_specs=[any_space] * 13,
        out_specs=any_space,
        scratch_shapes=scratch,
        compiler_params=pltpu.CompilerParams(
            collective_id=0, has_side_effects=True, vmem_limit_bytes=67043328
        ),
        name="cg",
    )(
        right_side,
        conductivity,
        reaction,
        leaf_factor.reshape(8, 512, 512),
        leaf_w,
        leaf_skeleton.reshape(8, 64),
        device_factor[0, 0, 0],
        device_weight[0, 0, 0],
        device_skeleton.reshape(1, 256),
        column_factor[0, 0],
        column_weight[0, 0],
        column_skeleton.reshape(1, 128),
        top_factor,
    )


def solution(mesh):
    cells = P("gx", "gy", "gz")
    in_specs = (cells,) * 10 + (P("gx", "gy"), P("gx", "gy"), P(("gx", "gy"), None))
    return jax.shard_map(local, mesh=mesh, in_specs=in_specs, out_specs=cells, check_vma=False)
```

```python
import jax
import jax.numpy as jnp
from jax import lax
from jax.experimental import pallas as pl
from jax.experimental.pallas import tpu as pltpu
from jax.sharding import PartitionSpec as P

F32, BF16 = jnp.float32, jnp.bfloat16
MESH = pl.DeviceIdType.MESH
B = 16
N = 256
NPQ, NS = 16, 8
PIECE = N // NS


def split(value):
    high = value.astype(BF16)
    return high, (value - high.astype(F32)).astype(BF16)


def mm(a, b):
    return jnp.dot(a, b, preferred_element_type=F32)


def mm_nt(a, b):
    return lax.dot_general(a, b, (((1,), (1,)), ((), ())), preferred_element_type=F32)


def dot3(a, b, product=mm):
    a_high, a_low = split(a)
    b_high, b_low = split(b)
    return product(a_high, b_high) + product(a_high, b_low) + product(a_low, b_high)


def each(first, count, body):
    def step(i, carry):
        body(i)
        return carry

    lax.fori_loop(first, count, step, 0)


def box_of(b, lead):
    x, y, z = lax.div(b, 4), lax.rem(lax.div(b, 2), 2), lax.rem(b, 2)
    return (
        pl.ds(8 * x + lead, 8),
        pl.ds(8 * y + lead, 8),
        pl.ds(pl.multiple_of(8 * z, 8), 8),
        slice(None),
    )


def kernel(
    rhs_hbm,
    cond_hbm,
    react_hbm,
    leaf_hbm,
    leaf_w_hbm,
    leaf_s_hbm,
    dev_hbm,
    dev_w_hbm,
    dev_s_hbm,
    col_hbm,
    col_w_hbm,
    col_s_hbm,
    top_hbm,
    out_hbm,
    rhs,
    cond_raw,
    react_raw,
    leaf_s,
    dev_s,
    col_s,
    half,
    react,
    leaf,
    leaf_hi,
    leaf_lo,
    leaf_v,
    leaf_vt,
    leaf_v3,
    dev,
    dev_v,
    dev_vt,
    col,
    col_v,
    col_vt,
    up_c,
    down_c,
    top,
    top_hi,
    top_lo,
    field,
    image,
    dev_in,
    dev_out,
    up_t,
    gath,
    near,
    rs,
    ag,
    tg,
    ar1,
    ar2,
    zsend,
    zrecv,
    hzsend,
    hzrecv,
    loc_sem,
    out_sem,
    gath_s,
    gath_r,
    rs_s,
    rs_r,
    ag_s,
    ag_r,
    tg_s,
    tg_r,
    a1_s,
    a1_r,
    a2_s,
    a2_r,
    halo_s,
    halo_r,
    hh_s,
    hh_r,
):
    gx, gy, gz = lax.axis_index("gx"), lax.axis_index("gy"), lax.axis_index("gz")
    pq = gx * 4 + gy
    chip, core = lax.div(gz, 2), lax.rem(gz, 2)
    mate = gz + 1 - 2 * core
    inner = pl.ds(1, B)

    column_peers = [
        lax.rem(chip + j, 4) * 2 + (1 - core if other else core)
        for j, other in ((2, 0), (2, 1), (1, 0), (1, 1), (3, 0), (3, 1), (0, 1))
    ]
    offsets = [(i, j) for i in range(4) for j in range(4) if i or j]
    offsets.sort(key=lambda o: -min(o[0], 4 - o[0]) - min(o[1], 4 - o[1]))
    plane_peers = [(lax.rem(gx + i, 4), lax.rem(gy + j, 4)) for i, j in offsets]

    def local(i, src, dst):
        return pltpu.make_async_copy(src, dst, loc_sem.at[i])

    loads = [
        local(0, rhs_hbm.at[pl.ds(0, 8)], rhs.at[pl.ds(0, 8)]),
        local(1, leaf_w_hbm, leaf_v),
        local(2, dev_w_hbm, dev_v),
        local(3, col_w_hbm.at[pl.ds(pl.multiple_of(gz * 256, 256), 256)], col_v),
        local(4, cond_hbm, cond_raw),
        local(5, dev_hbm, dev),
        local(6, top_hbm, top),
        local(7, col_hbm, col),
        local(8, react_hbm, react_raw),
        local(17, leaf_s_hbm, leaf_s),
        local(18, dev_s_hbm, dev_s),
        local(19, col_s_hbm, col_s),
        local(20, rhs_hbm.at[pl.ds(8, 8)], rhs.at[pl.ds(8, 8)]),
    ]
    leaf_loads = [local(9 + b, leaf_hbm.at[b], leaf.at[b]) for b in range(4)]
    for copy in loads[9:12] + loads[1:4] + loads[:1] + loads[12:]:
        copy.start()

    barrier = pltpu.get_barrier_semaphore()

    for x, y in plane_peers:
        pl.semaphore_signal(barrier, inc=1, device_id={"gx": x, "gy": y}, device_id_type=MESH)
    for peer in column_peers:
        pl.semaphore_signal(barrier, inc=1, device_id={"gz": peer}, device_id_type=MESH)

    def remote(src, dst, send, recv, device):
        return pltpu.make_async_remote_copy(
            src_ref=src,
            dst_ref=dst,
            send_sem=send,
            recv_sem=recv,
            device_id=device,
            device_id_type=MESH,
        )

    def column_start(buf, send, recv, k):
        def body(peer):
            remote(
                buf.at[k, gz], buf.at[k, gz], send.at[k, peer], recv.at[k, gz], {"gz": peer}
            ).start()

        for peer in column_peers:
            body(peer)

    def column_wait(buf, send, recv, k):
        def body(peer):
            remote(
                buf.at[k, gz], buf.at[k, peer], send.at[k, peer], recv.at[k, peer], {"gz": peer}
            ).wait()

        for peer in column_peers:
            body(peer)

    def plane_start(buf, send, recv, k):
        def body(x, y):
            peer = x * 4 + y
            remote(
                buf.at[k, pq], buf.at[k, pq], send.at[k, peer], recv.at[k, pq], {"gx": x, "gy": y}
            ).start()

        for x, y in plane_peers:
            body(x, y)

    def plane_wait(buf, send, recv, k):
        def body(x, y):
            peer = x * 4 + y
            remote(
                buf.at[k, pq], buf.at[k, peer], send.at[k, peer], recv.at[k, peer], {"gx": x, "gy": y}
            ).wait()

        for x, y in plane_peers:
            body(x, y)

    sides = ((gx, 4, "gx"), (gy, 4, "gy"), (gz, NS, "gz"))

    def layers(array, zs, zr, halved):
        size = B // 2 if halved else B
        lower, upper = pl.ds(1, size), pl.ds(1 + B - size, size)
        z_lower, z_upper = pl.ds(0, size), pl.ds(B - size, size)
        return (
            ((array.at[B, lower], array.at[0, lower]), (array.at[1, upper], array.at[B + 1, upper])),
            ((array.at[lower, B], array.at[lower, 0]), (array.at[upper, 1], array.at[upper, B + 1])),
            ((zs.at[1, z_lower], zr.at[0, z_lower]), (zs.at[0, z_upper], zr.at[1, z_upper])),
        )

    def halo_copies(array, zs, zr, send, recv, halved=False):
        copies = []
        parts = layers(array, zs, zr, halved)
        for axis, ((place, extent, name), pairs) in enumerate(zip(sides, parts)):
            for way, (src, dst) in enumerate(pairs):
                there = place + 1 if way == 0 else place - 1
                exists = place < extent - 1 if way == 0 else place > 0
                arrives = place > 0 if way == 0 else place < extent - 1
                i = 2 * axis + way
                copies.append(
                    (remote(src, dst, send.at[i], recv.at[i], {name: there}), exists, arrives, dst)
                )
        return copies

    def halo_start(copies):
        for copy, exists, _, _ in copies:
            pl.when(exists)(copy.start)

    def halo_zero(copies):
        for _, _, arrives, dst in copies:

            @pl.when(jnp.logical_not(arrives))
            def _():
                dst[...] = jnp.zeros(dst.shape, F32)

    def halo_wait(copies):
        for copy, exists, arrives, _ in copies:
            pl.when(exists)(copy.wait_send)
            pl.when(arrives)(copy.wait_recv)

    def pack_z(array, zs):
        def body(x):
            zs[0, x] = array[x + 1, 1 : B + 1, 0, :]
            zs[1, x] = array[x + 1, 1 : B + 1, B - 1, :]

        each(0, B, body)

    hh = halo_copies(half, hzsend, hzrecv, hh_s, hh_r)
    halos = [
        halo_copies(field.at[k], zsend.at[k], zrecv.at[k], halo_s.at[k], halo_r.at[k], k == 1)
        for k in range(2)
    ]

    def restrict_all(src, k):
        def leaf_box(b):
            u_high, u_low = split(src[box_of(b, 0)].reshape(512, N))
            both = mm(leaf_vt[b], u_high)
            total = both[:64] + both[64:] + mm(leaf_vt[b, :64], u_low)
            dev_in[pl.ds(pl.multiple_of(b * 64, 64), 64), :] = total

        if k == 0:
            loads[0].wait()
            loads[4].start()
            loads[8].start()
        each(0, 4, leaf_box)
        if k == 0:
            loads[12].wait()
            for copy in leaf_loads[:2] + loads[6:7] + leaf_loads[2:] + loads[5:6] + loads[7:8]:
                copy.start()
        each(4, 8, leaf_box)
        up_t[k] = dot3(up_c[...], dev_in[...]).T
        rs[k, gz] = up_t[k, pl.ds(pl.multiple_of(gz * PIECE, PIECE), PIECE), :]

    def rs_start(k):
        def body(peer):
            remote(
                up_t.at[k, pl.ds(pl.multiple_of(peer * PIECE, PIECE), PIECE)],
                rs.at[k, gz],
                rs_s.at[k, peer],
                rs_r.at[k, gz],
                {"gz": peer},
            ).start()

        for peer in column_peers:
            body(peer)

    def rs_wait(k):
        def body(peer):
            remote(
                up_t.at[k, pl.ds(pl.multiple_of(peer * PIECE, PIECE), PIECE)],
                rs.at[k, peer],
                rs_s.at[k, peer],
                rs_r.at[k, peer],
                {"gz": peer},
            ).wait()

        for peer in column_peers:
            body(peer)

    plus, minus, far = [lax.rem(chip + j, 4) * 2 + core for j in (1, 3, 2)]

    def half_block(k, slot, part, sem, to):
        ref = gath.at[k, slot, pl.ds(part * 128, 128)]
        return remote(ref, ref, gath_s.at[k, sem], gath_r.at[k, slot, part], {"gz": to})

    def gath_own(k):
        return [
            half_block(k, gz, part, sem, to)
            for sem, (part, to) in enumerate(
                ((0, plus), (1, minus), (1, plus), (0, minus), (0, mate), (1, mate))
            )
        ]

    def gath_onward(k):
        return [
            half_block(k, slot, part, 6 + sem, to)
            for sem, (slot, part, to) in enumerate(
                (
                    (minus, 0, plus),
                    (plus, 1, minus),
                    (minus, 0, mate),
                    (plus, 1, mate),
                    (minus, 1, mate),
                    (plus, 0, mate),
                    (far, 0, mate),
                    (far, 1, mate),
                )
            )
        ]

    def gath_wait(k, slot):
        for part in range(2):
            half_block(k, slot, part, 0, mate).wait_recv()

    def near_block(k, slot, first=False):
        columns = pl.ds(pl.multiple_of(slot * 256, 256), 256)
        value = dot3(col[:, columns], gath[k, slot])
        near[...] = value if first else near[...] + value

    def leaf_products(src, k, first, last):
        def body(b):
            u_high, u_low = split(src[box_of(b, 0)].reshape(512, N))
            if k == 0:
                slot = lax.rem(b, 4)
                pltpu.make_async_copy(leaf_hbm.at[b], leaf.at[slot], loc_sem.at[9 + b]).wait()
                high, low = split(leaf[slot])
                leaf_hi[b] = high
                leaf_lo[b] = low

                @pl.when(b < 4)
                def _():
                    pltpu.make_async_copy(
                        leaf_hbm.at[b + 4], leaf.at[slot], loc_sem.at[13 + b]
                    ).start()

            else:
                high, low = leaf_hi[b], leaf_lo[b]
            total = mm(high, u_high) + mm(high, u_low) + mm(low, u_high)
            field[(k,) + box_of(b, 1)] = total.reshape(8, 8, 8, N)

        each(first, last, body)

    def precondition(src, k, middle, later):
        restrict_all(src, k)
        if k == 0:
            pl.semaphore_wait(barrier, NS - 1 + NPQ - 1)
        rs_start(k)
        gath[k, gz] = dot3(dev_vt[...], dev_in[...])
        own, onward = gath_own(k), gath_onward(k)
        for copy in own:
            copy.start()
        middle()
        leaf_products(src, k, 0, 3)
        rs_wait(k)
        total = rs[k, 0]
        for i in range(1, NS):
            total = total + rs[k, i]
        ag[k, pq] = total
        plane_start(ag, ag_s, ag_r, k)
        leaf_products(src, k, 3, 5)
        for i in (0, 1):
            onward[2 + i].wait_recv()
            onward[i].start()
            onward[2 + i].start()
        if k == 0:
            loads[6].wait()
            top_hi[...], top_lo[...] = split(top[...])
        leaf_products(src, k, 5, 6)
        plane_wait(ag, ag_s, ag_r, k)
        tops = jnp.concatenate([ag[k, i] for i in range(NPQ)], axis=1)
        high, low = split(tops)
        rows = jnp.concatenate([high, low], axis=0)
        both = mm_nt(rows, top_hi[...])
        tg[k, gz] = both[:PIECE] + both[PIECE:] + mm_nt(high, top_lo[...])
        column_start(tg, tg_s, tg_r, k)
        for i in (4, 5):
            onward[i].wait_recv()
            onward[i].start()
        leaf_products(src, k, 6, 8)
        for i in (6, 7):
            onward[i].wait_recv()
            onward[i].start()
        if k == 0:
            loads[5].wait()
            loads[7].wait()
        dev_out[...] = dot3(dev[...], dev_in[...])
        later()
        near_block(k, gz, True)
        for slot in (minus, plus, far):
            near_block(k, slot)
        for base in (gz, minus, plus, far):
            slot = base + mate - gz
            gath_wait(k, slot)
            near_block(k, slot)
        dev_out[...] += dot3(dev_v[...], near[...])
        column_wait(tg, tg_s, tg_r, k)
        dev_out[...] += dot3(down_c[...], tg[k].reshape(N, 128), mm_nt)
        for copy in own + onward:
            copy.wait_send()

    def lift_boxes(k, finish):
        def body(b):
            high, low = split(dev_out[pl.ds(pl.multiple_of(b * 64, 64), 64), :])
            stacked = jnp.concatenate([high, low, high, jnp.zeros_like(high)], axis=0)
            place = (k,) + box_of(b, 1)
            total = field[place].reshape(512, N) + mm(leaf_v3[b], stacked)
            finish(b, place, total.reshape(8, 8, 8, N))

        each(0, 8, body)

    def twice(value):
        return jnp.concatenate([value, value], axis=1)

    def stencil(k, use):
        rows = lax.broadcasted_iota(jnp.int32, (B, 128), 0)
        first, last = rows == 0, rows == B - 1

        def body(x, carry):
            energy, curve = carry
            has_low = jnp.where(x > 0, 1.0, 0.0).astype(F32)
            has_high = jnp.where(x < B - 1, 1.0, 0.0).astype(F32)
            x_low, x_high = jnp.maximum(x, 1), jnp.minimum(x + 2, B)
            for y in range(B):
                v = field[k, x + 1, y + 1]
                h = half[x + 1, y + 1]
                if k == 1:
                    face_up = jnp.where(last, 0.0, h + pltpu.roll(h, B - 1, 0))
                    face_xh = (h + half[x + 2, y + 1]) * has_high
                    applied = (
                        twice(0.5 * react[x, y]) * v
                        - twice(face_xh) * field[k, x_high, y + 1]
                        - twice(face_up) * pltpu.roll(v, B - 1, 0)
                    )
                    if y < B - 1:
                        face_yh = h + half[x + 1, y + 2]
                        applied = applied - twice(face_yh) * field[k, x + 1, y + 2]
                    energy = energy + use(x, y, None) * v
                    curve = curve + v * applied
                    continue
                low, high = hzrecv[0, x, y : y + 1, :], hzrecv[1, x, y : y + 1, :]
                face_up = h + jnp.where(last, high, pltpu.roll(h, B - 1, 0))
                face_down = h + jnp.where(first, low, pltpu.roll(h, 1, 0))
                face_xl, face_xh = h + half[x, y + 1], h + half[x + 2, y + 1]
                face_yl = h + half[x + 1, y] if y == 0 else face_yh
                face_yh = h + half[x + 1, y + 2]
                total = react[x, y] + face_up + face_down + face_xl + face_xh + face_yl + face_yh
                react[x, y] = total
                applied = (
                    twice(total) * v
                    - twice(face_xl * has_low) * field[k, x_low, y + 1]
                    - twice(face_xh * has_high) * field[k, x_high, y + 1]
                    - twice(jnp.where(last, 0.0, face_up)) * pltpu.roll(v, B - 1, 0)
                    - twice(jnp.where(first, 0.0, face_down)) * pltpu.roll(v, 1, 0)
                )
                if y > 0:
                    applied = applied - twice(face_yl) * field[k, x + 1, y]
                if y < B - 1:
                    applied = applied - twice(face_yh) * field[k, x + 1, y + 2]
                energy = energy + use(x, y, applied) * v
                curve = curve + v * applied
            return energy, curve

        zero = jnp.zeros((B, N), F32)
        return lax.fori_loop(0, B, body, (zero, zero))

    def outer_terms(k, curve):
        def body(i, total):
            for side in range(2):
                at = i + B // 2 * side if k == 1 else i
                edge, beyond = (1, 0) if side == 0 else (B, B + 1)
                part = twice(half[edge, at + 1] + half[beyond, at + 1]) * field[k, beyond, at + 1]
                total = total + part * field[k, edge, at + 1]
                if k == 0:
                    image[edge - 1, at] -= part
                part = twice(half[at + 1, edge] + half[at + 1, beyond]) * field[k, at + 1, beyond]
                total = total + part * field[k, at + 1, edge]
                if k == 0:
                    image[at, edge - 1] -= part
                part = twice(hzsend[side, at] + hzrecv[side, at]) * zrecv[k, side, at]
                total = total + part * zsend[k, side, at]
                if k == 0:
                    image[at, :, edge - 1, :] -= part
            return total

        count = B // 2 if k == 1 else B
        total = lax.fori_loop(0, count, body, jnp.zeros((B, N), F32))
        return 2.0 * (curve - total) if k == 1 else curve - total

    def ar_first(k, energy, curve):
        row = lax.broadcasted_iota(jnp.int32, (8, 128), 0)
        e = jnp.sum(energy, axis=0, keepdims=True)
        c = jnp.sum(curve, axis=0, keepdims=True)
        packed = jnp.where(row == 3, c[:, 128:], 0.0)
        for i, line in enumerate((e[:, :128], e[:, 128:], c[:, :128])):
            packed = jnp.where(row == i, line, packed)
        ar1[k, gz] = packed
        column_start(ar1, a1_s, a1_r, k)

    def ar_second(k):
        column_wait(ar1, a1_s, a1_r, k)
        total = ar1[k, 0]
        for i in range(1, NS):
            total = total + ar1[k, i]
        ar2[k, pq] = total
        plane_start(ar2, a2_s, a2_r, k)

    def ar_third(k):
        plane_wait(ar2, a2_s, a2_r, k)
        total = ar2[k, 0]
        for i in range(1, NPQ):
            total = total + ar2[k, i]
        lines = [total[i : i + 1] for i in range(4)]
        return jnp.concatenate(lines[:2], axis=1), jnp.concatenate(lines[2:], axis=1)

    for i in (1, 9, 10, 11):
        loads[i].wait()
    padded = jnp.concatenate([leaf_s[...], jnp.zeros((8, 64), jnp.int32)], axis=1).astype(F32)
    numbers = padded.T[:64]
    chosen_box = lax.broadcasted_iota(jnp.int32, (64, 8), 1)
    places = lax.broadcasted_iota(jnp.int32, (64, 512), 1).astype(F32)

    def prepare(b):
        mine = jnp.sum(jnp.where(chosen_box == b, numbers, 0.0), axis=1, keepdims=True)
        high, low = split(leaf_v[b] + jnp.where(places == mine, 1.0, 0.0))
        leaf_vt[b] = jnp.concatenate([high, low], axis=0)
        high, low = high.astype(F32), low.astype(F32)
        leaf_v3[b] = jnp.concatenate([high, high, low, jnp.zeros_like(low)], axis=0).T.astype(BF16)

    each(0, 8, prepare)
    loads[2].wait()
    rows = lax.broadcasted_iota(jnp.int32, (512, 256), 0)
    dev_v[...] += jnp.where(rows == dev_s[...], 1.0, 0.0)
    dev_vt[...] = dev_v[...].T
    loads[3].wait()
    rows = lax.broadcasted_iota(jnp.int32, (256, 128), 0) + gz * 256
    col_v[...] += jnp.where(rows == col_s[...], 1.0, 0.0)
    col_vt[...] = col_v[...].T
    up_c[...] = dot3(col_vt[...], dev_vt[...])

    for copies in [hh] + halos:
        halo_zero(copies)

    def send_halves():
        loads[4].wait()
        loads[8].wait()
        diagonal = lax.broadcasted_iota(jnp.int32, (B, B), 0) == lax.broadcasted_iota(
            jnp.int32, (B, B), 1
        )

        def spread(line):
            value = jnp.sum(jnp.where(diagonal, line, 0.0), axis=1, keepdims=True)
            return jnp.broadcast_to(value, (B, 128))

        def body(x):
            for y in range(B):
                half[x + 1, y + 1] = 0.5 * spread(cond_raw[x, y : y + 1, :])
                react[x, y] = spread(react_raw[x, y : y + 1, :])

        each(0, B, body)
        pack_z(half, hzsend)
        halo_start(hh)
        down_c[...] = dot3(dev_v[...], col_v[...])

    precondition(rhs, 0, send_halves, lambda: None)

    def keep(b, place, total):
        field[place] = total

    lift_boxes(0, keep)
    pack_z(field.at[0], zsend.at[0])
    halo_start(halos[0])
    halo_wait(hh)

    def use_first(x, y, applied):
        image[x, y] = applied
        return rhs[x, y]

    energy, curve = stencil(0, use_first)
    halo_wait(halos[0])
    curve = outer_terms(0, curve)
    ar_first(0, energy, curve)

    precondition(image, 1, lambda: ar_second(0), lambda: None)
    energy0, curve0 = ar_third(0)
    step0 = energy0 / curve0

    def subtract(b, place, total):
        field[place] = field[(0,) + place[1:]] - step0.reshape(1, 1, 1, N) * total

    lift_boxes(1, subtract)
    pack_z(field.at[1], zsend.at[1])
    halo_start(halos[1])

    def use_second(x, y, applied):
        return rhs[x, y] - step0 * image[x, y]

    energy, curve = stencil(1, use_second)
    halo_wait(halos[1])
    curve = outer_terms(1, curve)
    ar_first(1, energy, curve)
    ar_second(1)
    energy1, curve1 = ar_third(1)
    mixing = energy1 / energy0
    step1 = energy1 / (curve1 - mixing * energy1 / step0)
    ahead = (step0 + step1 * mixing).reshape(1, 1, N)
    last = step1.reshape(1, 1, N)

    def write(x):
        image[x] = ahead * field[0, x + 1, 1 : B + 1] + last * field[1, x + 1, 1 : B + 1]
        pltpu.make_async_copy(image.at[x], out_hbm.at[x], out_sem.at[x]).start()

    each(0, B, write)

    def written(x):
        pltpu.make_async_copy(image.at[x], out_hbm.at[x], out_sem.at[x]).wait()

    each(0, B, written)


def local(
    right_side,
    conductivity,
    reaction,
    leaf_factor,
    leaf_weight,
    leaf_skeleton,
    device_factor,
    device_weight,
    device_skeleton,
    column_factor,
    column_weight,
    column_skeleton,
    top_factor,
):
    leaf_w = jnp.swapaxes(leaf_weight.reshape(8, 512, 64), 1, 2)
    any_space = pl.BlockSpec(memory_space=pl.ANY)
    dma = pltpu.SemaphoreType.DMA
    vm = pltpu.VMEM
    scratch = [
        vm((B, B, B, N), F32),
        vm((B, B, B), F32),
        vm((B, B, B), F32),
        vm((8, 64), jnp.int32),
        vm((1, 256), jnp.int32),
        vm((1, 128), jnp.int32),
        vm((B + 2, B + 2, B, 128), F32),
        vm((B, B, B, 128), F32),
        vm((4, 512, 512), F32),
        vm((8, 512, 512), BF16),
        vm((8, 512, 512), BF16),
        vm((8, 64, 512), F32),
        vm((8, 128, 512), BF16),
        vm((8, 512, 256), BF16),
        vm((512, 512), F32),
        vm((512, 256), F32),
        vm((256, 512), F32),
        vm((256, 2048), F32),
        vm((256, 128), F32),
        vm((128, 256), F32),
        vm((128, 512), F32),
        vm((512, 128), F32),
        vm((128, 2048), F32),
        vm((128, 2048), BF16),
        vm((128, 2048), BF16),
        vm((2, B + 2, B + 2, B, N), F32),
        vm((B, B, B, N), F32),
        vm((512, N), F32),
        vm((512, N), F32),
        vm((2, N, 128), F32),
        vm((2, NS, 256, N), F32),
        vm((256, N), F32),
        vm((2, NS, PIECE, 128), F32),
        vm((2, NPQ, PIECE, 128), F32),
        vm((2, NS, PIECE, 128), F32),
        vm((2, NS, 8, 128), F32),
        vm((2, NPQ, 8, 128), F32),
        vm((2, 2, B, B, N), F32),
        vm((2, 2, B, B, N), F32),
        vm((2, B, B, 128), F32),
        vm((2, B, B, 128), F32),
        dma((21,)),
        dma((B,)),
        dma((2, 14)),
        dma((2, NS, 2)),
        dma((2, NS)),
        dma((2, NS)),
        dma((2, NPQ)),
        dma((2, NPQ)),
        dma((2, NS)),
        dma((2, NS)),
        dma((2, NS)),
        dma((2, NS)),
        dma((2, NPQ)),
        dma((2, NPQ)),
        dma((2, 6)),
        dma((2, 6)),
        dma((6,)),
        dma((6,)),
    ]
    return pl.pallas_call(
        kernel,
        out_shape=jax.ShapeDtypeStruct((B, B, B, N), F32),
        in_specs=[any_space] * 13,
        out_specs=any_space,
        scratch_shapes=scratch,
        compiler_params=pltpu.CompilerParams(
            collective_id=0, has_side_effects=True, vmem_limit_bytes=67043328
        ),
        name="cg",
    )(
        right_side,
        conductivity,
        reaction,
        leaf_factor.reshape(8, 512, 512),
        leaf_w,
        leaf_skeleton.reshape(8, 64),
        device_factor[0, 0, 0],
        device_weight[0, 0, 0],
        device_skeleton.reshape(1, 256),
        column_factor[0, 0],
        column_weight[0, 0],
        column_skeleton.reshape(1, 128),
        top_factor,
    )


def solution(mesh):
    cells = P("gx", "gy", "gz")
    in_specs = (cells,) * 10 + (P("gx", "gy"), P("gx", "gy"), P(("gx", "gy"), None))
    return jax.shard_map(local, mesh=mesh, in_specs=in_specs, out_specs=cells, check_vma=False)
```

```python
import jax
import jax.numpy as jnp
from jax import lax
from jax.experimental import pallas as pl
from jax.experimental.pallas import tpu as pltpu
from jax.sharding import PartitionSpec as P

F32, BF16 = jnp.float32, jnp.bfloat16
MESH = pl.DeviceIdType.MESH
B = 16
N = 256
NPQ, NS = 16, 8
PIECE = N // NS


def split(value):
    high = value.astype(BF16)
    return high, (value - high.astype(F32)).astype(BF16)


def mm(a, b):
    return jnp.dot(a, b, preferred_element_type=F32)


def mm_nt(a, b):
    return lax.dot_general(a, b, (((1,), (1,)), ((), ())), preferred_element_type=F32)


def dot3(a, b, product=mm):
    a_high, a_low = split(a)
    b_high, b_low = split(b)
    return product(a_high, b_high) + product(a_high, b_low) + product(a_low, b_high)


def each(first, count, body):
    def step(i, carry):
        body(i)
        return carry

    lax.fori_loop(first, count, step, 0)


def box_of(b, lead):
    x, y, z = lax.div(b, 4), lax.rem(lax.div(b, 2), 2), lax.rem(b, 2)
    return (
        pl.ds(8 * x + lead, 8),
        pl.ds(8 * y + lead, 8),
        pl.ds(pl.multiple_of(8 * z, 8), 8),
        slice(None),
    )


def kernel(
    rhs_hbm,
    cond_hbm,
    react_hbm,
    leaf_hbm,
    leaf_w_hbm,
    leaf_s_hbm,
    dev_hbm,
    dev_w_hbm,
    dev_s_hbm,
    col_hbm,
    col_w_hbm,
    col_s_hbm,
    top_hbm,
    out_hbm,
    rhs,
    cond_raw,
    react_raw,
    leaf_s,
    dev_s,
    col_s,
    half,
    react,
    leaf,
    leaf_hi,
    leaf_lo,
    leaf_v,
    leaf_vt,
    leaf_v3,
    dev,
    dev_v,
    dev_vt,
    col,
    col_v,
    col_vt,
    up_c,
    down_c,
    top,
    top_hi,
    top_lo,
    field,
    image,
    dev_in,
    dev_out,
    up_t,
    gath,
    near,
    rs,
    ag,
    tg,
    ar1,
    ar2,
    zsend,
    zrecv,
    hzsend,
    hzrecv,
    loc_sem,
    out_sem,
    gath_s,
    gath_r,
    rs_s,
    rs_r,
    ag_s,
    ag_r,
    tg_s,
    tg_r,
    a1_s,
    a1_r,
    a2_s,
    a2_r,
    halo_s,
    halo_r,
    hh_s,
    hh_r,
):
    gx, gy, gz = lax.axis_index("gx"), lax.axis_index("gy"), lax.axis_index("gz")
    pq = gx * 4 + gy
    chip, core = lax.div(gz, 2), lax.rem(gz, 2)
    mate = gz + 1 - 2 * core
    inner = pl.ds(1, B)

    column_peers = [
        lax.rem(chip + j, 4) * 2 + (1 - core if other else core)
        for j, other in ((2, 0), (2, 1), (1, 0), (1, 1), (3, 0), (3, 1), (0, 1))
    ]
    offsets = [(i, j) for i in range(4) for j in range(4) if i or j]
    offsets.sort(key=lambda o: -min(o[0], 4 - o[0]) - min(o[1], 4 - o[1]))
    plane_peers = [(lax.rem(gx + i, 4), lax.rem(gy + j, 4)) for i, j in offsets]

    def local(i, src, dst):
        return pltpu.make_async_copy(src, dst, loc_sem.at[i])

    loads = [
        local(0, rhs_hbm.at[pl.ds(0, 8)], rhs.at[pl.ds(0, 8)]),
        local(1, leaf_w_hbm, leaf_v),
        local(2, dev_w_hbm, dev_v),
        local(3, col_w_hbm.at[pl.ds(pl.multiple_of(gz * 256, 256), 256)], col_v),
        local(4, cond_hbm, cond_raw),
        local(5, dev_hbm, dev),
        local(6, top_hbm, top),
        local(7, col_hbm, col),
        local(8, react_hbm, react_raw),
        local(17, leaf_s_hbm, leaf_s),
        local(18, dev_s_hbm, dev_s),
        local(19, col_s_hbm, col_s),
        local(20, rhs_hbm.at[pl.ds(8, 8)], rhs.at[pl.ds(8, 8)]),
    ]
    leaf_loads = [local(9 + b, leaf_hbm.at[b], leaf.at[b]) for b in range(4)]
    for copy in loads[9:12] + loads[1:4] + loads[:1] + loads[12:]:
        copy.start()

    barrier = pltpu.get_barrier_semaphore()

    for x, y in plane_peers:
        pl.semaphore_signal(barrier, inc=1, device_id={"gx": x, "gy": y}, device_id_type=MESH)
    for peer in column_peers:
        pl.semaphore_signal(barrier, inc=1, device_id={"gz": peer}, device_id_type=MESH)

    def remote(src, dst, send, recv, device):
        return pltpu.make_async_remote_copy(
            src_ref=src,
            dst_ref=dst,
            send_sem=send,
            recv_sem=recv,
            device_id=device,
            device_id_type=MESH,
        )

    def column_start(buf, send, recv, k):
        def body(peer):
            remote(
                buf.at[k, gz], buf.at[k, gz], send.at[k, peer], recv.at[k, gz], {"gz": peer}
            ).start()

        for peer in column_peers:
            body(peer)

    def column_wait(buf, send, recv, k, sent=False):
        def body(peer):
            copy = remote(
                buf.at[k, gz], buf.at[k, peer], send.at[k, peer], recv.at[k, peer], {"gz": peer}
            )
            if sent:
                copy.wait_send()
            else:
                copy.wait_recv()

        for peer in column_peers:
            body(peer)

    def plane_start(buf, send, recv, k):
        def body(x, y):
            peer = x * 4 + y
            remote(
                buf.at[k, pq], buf.at[k, pq], send.at[k, peer], recv.at[k, pq], {"gx": x, "gy": y}
            ).start()

        for x, y in plane_peers:
            body(x, y)

    def plane_wait(buf, send, recv, k, sent=False):
        def body(x, y):
            peer = x * 4 + y
            copy = remote(
                buf.at[k, pq], buf.at[k, peer], send.at[k, peer], recv.at[k, peer], {"gx": x, "gy": y}
            )
            if sent:
                copy.wait_send()
            else:
                copy.wait_recv()

        for x, y in plane_peers:
            body(x, y)

    sides = ((gx, 4, "gx"), (gy, 4, "gy"), (gz, NS, "gz"))

    def layers(array, zs, zr, halved):
        size = B // 2 if halved else B
        lower, upper = pl.ds(1, size), pl.ds(1 + B - size, size)
        z_lower, z_upper = pl.ds(0, size), pl.ds(B - size, size)
        return (
            ((array.at[B, lower], array.at[0, lower]), (array.at[1, upper], array.at[B + 1, upper])),
            ((array.at[lower, B], array.at[lower, 0]), (array.at[upper, 1], array.at[upper, B + 1])),
            ((zs.at[1, z_lower], zr.at[0, z_lower]), (zs.at[0, z_upper], zr.at[1, z_upper])),
        )

    def halo_copies(array, zs, zr, send, recv, halved=False):
        copies = []
        parts = layers(array, zs, zr, halved)
        for axis, ((place, extent, name), pairs) in enumerate(zip(sides, parts)):
            for way, (src, dst) in enumerate(pairs):
                there = place + 1 if way == 0 else place - 1
                exists = place < extent - 1 if way == 0 else place > 0
                arrives = place > 0 if way == 0 else place < extent - 1
                i = 2 * axis + way
                copies.append(
                    (remote(src, dst, send.at[i], recv.at[i], {name: there}), exists, arrives, dst)
                )
        return copies

    def halo_start(copies):
        for copy, exists, _, _ in copies:
            pl.when(exists)(copy.start)

    def halo_zero(copies):
        for _, _, arrives, dst in copies:

            @pl.when(jnp.logical_not(arrives))
            def _():
                dst[...] = jnp.zeros(dst.shape, F32)

    def halo_wait(copies):
        for copy, exists, arrives, _ in copies:
            pl.when(arrives)(copy.wait_recv)

    def pack_z(array, zs):
        def body(x):
            zs[0, x] = array[x + 1, 1 : B + 1, 0, :]
            zs[1, x] = array[x + 1, 1 : B + 1, B - 1, :]

        each(0, B, body)

    hh = halo_copies(half, hzsend, hzrecv, hh_s, hh_r)
    halos = [
        halo_copies(field.at[k], zsend.at[k], zrecv.at[k], halo_s.at[k], halo_r.at[k], k == 1)
        for k in range(2)
    ]

    def restrict_all(src, k):
        def leaf_box(b):
            u_high, u_low = split(src[box_of(b, 0)].reshape(512, N))
            both = mm(leaf_vt[b], u_high)
            total = both[:64] + both[64:] + mm(leaf_vt[b, :64], u_low)
            dev_in[pl.ds(pl.multiple_of(b * 64, 64), 64), :] = total

        if k == 0:
            loads[0].wait()
            loads[4].start()
            loads[8].start()
        each(0, 4, leaf_box)
        if k == 0:
            loads[12].wait()
            for copy in leaf_loads[:2] + loads[6:7] + leaf_loads[2:] + loads[5:6] + loads[7:8]:
                copy.start()
        each(4, 8, leaf_box)
        up_t[k] = dot3(up_c[...], dev_in[...]).T
        rs[k, gz] = up_t[k, pl.ds(pl.multiple_of(gz * PIECE, PIECE), PIECE), :]

    def rs_start(k):
        def body(peer):
            remote(
                up_t.at[k, pl.ds(pl.multiple_of(peer * PIECE, PIECE), PIECE)],
                rs.at[k, gz],
                rs_s.at[k, peer],
                rs_r.at[k, gz],
                {"gz": peer},
            ).start()

        for peer in column_peers:
            body(peer)

    def rs_wait(k, sent=False):
        def body(peer):
            copy = remote(
                up_t.at[k, pl.ds(pl.multiple_of(peer * PIECE, PIECE), PIECE)],
                rs.at[k, peer],
                rs_s.at[k, peer],
                rs_r.at[k, peer],
                {"gz": peer},
            )
            if sent:
                copy.wait_send()
            else:
                copy.wait_recv()

        for peer in column_peers:
            body(peer)

    plus, minus, far = [lax.rem(chip + j, 4) * 2 + core for j in (1, 3, 2)]

    def half_block(k, slot, part, sem, to):
        ref = gath.at[k, slot, pl.ds(part * 128, 128)]
        return remote(ref, ref, gath_s.at[k, sem], gath_r.at[k, slot, part], {"gz": to})

    def gath_own(k):
        return [
            half_block(k, gz, part, sem, to)
            for sem, (part, to) in enumerate(
                ((0, plus), (1, minus), (1, plus), (0, minus), (0, mate), (1, mate))
            )
        ]

    def gath_onward(k):
        return [
            half_block(k, slot, part, 6 + sem, to)
            for sem, (slot, part, to) in enumerate(
                (
                    (minus, 0, plus),
                    (plus, 1, minus),
                    (minus, 0, mate),
                    (plus, 1, mate),
                    (minus, 1, mate),
                    (plus, 0, mate),
                    (far, 0, mate),
                    (far, 1, mate),
                )
            )
        ]

    def gath_wait(k, slot):
        for part in range(2):
            half_block(k, slot, part, 0, mate).wait_recv()

    def near_block(k, slot, first=False):
        columns = pl.ds(pl.multiple_of(slot * 256, 256), 256)
        value = dot3(col[:, columns], gath[k, slot])
        near[...] = value if first else near[...] + value

    def leaf_products(src, k, first, last):
        def body(b):
            u_high, u_low = split(src[box_of(b, 0)].reshape(512, N))
            if k == 0:
                slot = lax.rem(b, 4)
                pltpu.make_async_copy(leaf_hbm.at[b], leaf.at[slot], loc_sem.at[9 + b]).wait()
                high, low = split(leaf[slot])
                leaf_hi[b] = high
                leaf_lo[b] = low

                @pl.when(b < 4)
                def _():
                    pltpu.make_async_copy(
                        leaf_hbm.at[b + 4], leaf.at[slot], loc_sem.at[13 + b]
                    ).start()

            else:
                high, low = leaf_hi[b], leaf_lo[b]
            total = mm(high, u_high) + mm(high, u_low) + mm(low, u_high)
            field[(k,) + box_of(b, 1)] = total.reshape(8, 8, 8, N)

        each(first, last, body)

    unsent = []

    def precondition(src, k, middle, later):
        restrict_all(src, k)
        if k == 0:
            pl.semaphore_wait(barrier, NS - 1 + NPQ - 1)
        rs_start(k)
        gath[k, gz] = dot3(dev_vt[...], dev_in[...])
        own, onward = gath_own(k), gath_onward(k)
        for copy in own:
            copy.start()
        middle()
        leaf_products(src, k, 0, 3)
        rs_wait(k)
        total = rs[k, 0]
        for i in range(1, NS):
            total = total + rs[k, i]
        ag[k, pq] = total
        plane_start(ag, ag_s, ag_r, k)
        leaf_products(src, k, 3, 5)
        for i in (0, 1):
            onward[2 + i].wait_recv()
            onward[i].start()
            onward[2 + i].start()
        if k == 0:
            loads[6].wait()
            top_hi[...], top_lo[...] = split(top[...])
        leaf_products(src, k, 5, 6)
        plane_wait(ag, ag_s, ag_r, k)
        tops = jnp.concatenate([ag[k, i] for i in range(NPQ)], axis=1)
        high, low = split(tops)
        rows = jnp.concatenate([high, low], axis=0)
        both = mm_nt(rows, top_hi[...])
        tg[k, gz] = both[:PIECE] + both[PIECE:] + mm_nt(high, top_lo[...])
        column_start(tg, tg_s, tg_r, k)
        for i in (4, 5):
            onward[i].wait_recv()
            onward[i].start()
        leaf_products(src, k, 6, 8)
        for i in (6, 7):
            onward[i].wait_recv()
            onward[i].start()
        if k == 0:
            loads[5].wait()
            loads[7].wait()
        dev_out[...] = dot3(dev[...], dev_in[...])
        later()
        near_block(k, gz, True)
        for slot in (minus, plus, far):
            near_block(k, slot)
        for base in (gz, minus, plus, far):
            slot = base + mate - gz
            gath_wait(k, slot)
            near_block(k, slot)
        dev_out[...] += dot3(dev_v[...], near[...])
        column_wait(tg, tg_s, tg_r, k)
        dev_out[...] += dot3(down_c[...], tg[k].reshape(N, 128), mm_nt)
        unsent.extend(own + onward)

    def lift_boxes(k, finish):
        def body(b):
            high, low = split(dev_out[pl.ds(pl.multiple_of(b * 64, 64), 64), :])
            stacked = jnp.concatenate([high, low, high, jnp.zeros_like(high)], axis=0)
            place = (k,) + box_of(b, 1)
            total = field[place].reshape(512, N) + mm(leaf_v3[b], stacked)
            finish(b, place, total.reshape(8, 8, 8, N))

        each(0, 8, body)

    def twice(value):
        return jnp.concatenate([value, value], axis=1)

    def stencil(k, use):
        rows = lax.broadcasted_iota(jnp.int32, (B, 128), 0)
        first, last = rows == 0, rows == B - 1

        def body(x, carry):
            energy, curve = carry
            has_low = jnp.where(x > 0, 1.0, 0.0).astype(F32)
            has_high = jnp.where(x < B - 1, 1.0, 0.0).astype(F32)
            x_low, x_high = jnp.maximum(x, 1), jnp.minimum(x + 2, B)
            for y in range(B):
                v = field[k, x + 1, y + 1]
                h = half[x + 1, y + 1]
                if k == 1:
                    face_up = jnp.where(last, 0.0, h + pltpu.roll(h, B - 1, 0))
                    face_xh = (h + half[x + 2, y + 1]) * has_high
                    applied = (
                        twice(0.5 * react[x, y]) * v
                        - twice(face_xh) * field[k, x_high, y + 1]
                        - twice(face_up) * pltpu.roll(v, B - 1, 0)
                    )
                    if y < B - 1:
                        face_yh = h + half[x + 1, y + 2]
                        applied = applied - twice(face_yh) * field[k, x + 1, y + 2]
                    energy = energy + use(x, y, None) * v
                    curve = curve + v * applied
                    continue
                low, high = hzrecv[0, x, y : y + 1, :], hzrecv[1, x, y : y + 1, :]
                face_up = h + jnp.where(last, high, pltpu.roll(h, B - 1, 0))
                face_down = h + jnp.where(first, low, pltpu.roll(h, 1, 0))
                face_xl, face_xh = h + half[x, y + 1], h + half[x + 2, y + 1]
                face_yl = h + half[x + 1, y] if y == 0 else face_yh
                face_yh = h + half[x + 1, y + 2]
                total = react[x, y] + face_up + face_down + face_xl + face_xh + face_yl + face_yh
                react[x, y] = total
                applied = (
                    twice(total) * v
                    - twice(face_xl * has_low) * field[k, x_low, y + 1]
                    - twice(face_xh * has_high) * field[k, x_high, y + 1]
                    - twice(jnp.where(last, 0.0, face_up)) * pltpu.roll(v, B - 1, 0)
                    - twice(jnp.where(first, 0.0, face_down)) * pltpu.roll(v, 1, 0)
                )
                if y > 0:
                    applied = applied - twice(face_yl) * field[k, x + 1, y]
                if y < B - 1:
                    applied = applied - twice(face_yh) * field[k, x + 1, y + 2]
                energy = energy + use(x, y, applied) * v
                curve = curve + v * applied
            return energy, curve

        zero = jnp.zeros((B, N), F32)
        return lax.fori_loop(0, B, body, (zero, zero))

    def outer_terms(k, curve):
        def body(i, total):
            for side in range(2):
                at = i + B // 2 * side if k == 1 else i
                edge, beyond = (1, 0) if side == 0 else (B, B + 1)
                part = twice(half[edge, at + 1] + half[beyond, at + 1]) * field[k, beyond, at + 1]
                total = total + part * field[k, edge, at + 1]
                if k == 0:
                    image[edge - 1, at] -= part
                part = twice(half[at + 1, edge] + half[at + 1, beyond]) * field[k, at + 1, beyond]
                total = total + part * field[k, at + 1, edge]
                if k == 0:
                    image[at, edge - 1] -= part
                part = twice(hzsend[side, at] + hzrecv[side, at]) * zrecv[k, side, at]
                total = total + part * zsend[k, side, at]
                if k == 0:
                    image[at, :, edge - 1, :] -= part
            return total

        count = B // 2 if k == 1 else B
        total = lax.fori_loop(0, count, body, jnp.zeros((B, N), F32))
        return 2.0 * (curve - total) if k == 1 else curve - total

    def ar_first(k, energy, curve):
        row = lax.broadcasted_iota(jnp.int32, (8, 128), 0)
        e = jnp.sum(energy, axis=0, keepdims=True)
        c = jnp.sum(curve, axis=0, keepdims=True)
        packed = jnp.where(row == 3, c[:, 128:], 0.0)
        for i, line in enumerate((e[:, :128], e[:, 128:], c[:, :128])):
            packed = jnp.where(row == i, line, packed)
        ar1[k, gz] = packed
        column_start(ar1, a1_s, a1_r, k)

    def ar_second(k):
        column_wait(ar1, a1_s, a1_r, k)
        total = ar1[k, 0]
        for i in range(1, NS):
            total = total + ar1[k, i]
        ar2[k, pq] = total
        plane_start(ar2, a2_s, a2_r, k)

    def ar_third(k):
        plane_wait(ar2, a2_s, a2_r, k)
        total = ar2[k, 0]
        for i in range(1, NPQ):
            total = total + ar2[k, i]
        lines = [total[i : i + 1] for i in range(4)]
        return jnp.concatenate(lines[:2], axis=1), jnp.concatenate(lines[2:], axis=1)

    for i in (1, 9, 10, 11):
        loads[i].wait()
    padded = jnp.concatenate([leaf_s[...], jnp.zeros((8, 64), jnp.int32)], axis=1).astype(F32)
    numbers = padded.T[:64]
    chosen_box = lax.broadcasted_iota(jnp.int32, (64, 8), 1)
    places = lax.broadcasted_iota(jnp.int32, (64, 512), 1).astype(F32)

    def prepare(b):
        mine = jnp.sum(jnp.where(chosen_box == b, numbers, 0.0), axis=1, keepdims=True)
        high, low = split(leaf_v[b] + jnp.where(places == mine, 1.0, 0.0))
        leaf_vt[b] = jnp.concatenate([high, low], axis=0)
        high, low = high.astype(F32), low.astype(F32)
        leaf_v3[b] = jnp.concatenate([high, high, low, jnp.zeros_like(low)], axis=0).T.astype(BF16)

    each(0, 8, prepare)
    loads[2].wait()
    rows = lax.broadcasted_iota(jnp.int32, (512, 256), 0)
    dev_v[...] += jnp.where(rows == dev_s[...], 1.0, 0.0)
    dev_vt[...] = dev_v[...].T
    loads[3].wait()
    rows = lax.broadcasted_iota(jnp.int32, (256, 128), 0) + gz * 256
    col_v[...] += jnp.where(rows == col_s[...], 1.0, 0.0)
    col_vt[...] = col_v[...].T
    up_c[...] = dot3(col_vt[...], dev_vt[...])

    for copies in [hh] + halos:
        halo_zero(copies)

    def send_halves():
        loads[4].wait()
        loads[8].wait()
        diagonal = lax.broadcasted_iota(jnp.int32, (B, B), 0) == lax.broadcasted_iota(
            jnp.int32, (B, B), 1
        )

        def spread(line):
            value = jnp.sum(jnp.where(diagonal, line, 0.0), axis=1, keepdims=True)
            return jnp.broadcast_to(value, (B, 128))

        def body(x):
            for y in range(B):
                half[x + 1, y + 1] = 0.5 * spread(cond_raw[x, y : y + 1, :])
                react[x, y] = spread(react_raw[x, y : y + 1, :])

        each(0, B, body)
        pack_z(half, hzsend)
        halo_start(hh)
        down_c[...] = dot3(dev_v[...], col_v[...])

    precondition(rhs, 0, send_halves, lambda: None)

    def keep(b, place, total):
        field[place] = total

    lift_boxes(0, keep)
    pack_z(field.at[0], zsend.at[0])
    halo_start(halos[0])
    halo_wait(hh)

    def use_first(x, y, applied):
        image[x, y] = applied
        return rhs[x, y]

    energy, curve = stencil(0, use_first)
    halo_wait(halos[0])
    curve = outer_terms(0, curve)
    ar_first(0, energy, curve)

    precondition(image, 1, lambda: ar_second(0), lambda: None)
    energy0, curve0 = ar_third(0)
    step0 = energy0 / curve0

    def subtract(b, place, total):
        field[place] = field[(0,) + place[1:]] - step0.reshape(1, 1, 1, N) * total

    lift_boxes(1, subtract)
    pack_z(field.at[1], zsend.at[1])
    halo_start(halos[1])

    def use_second(x, y, applied):
        return rhs[x, y] - step0 * image[x, y]

    energy, curve = stencil(1, use_second)
    halo_wait(halos[1])
    curve = outer_terms(1, curve)
    ar_first(1, energy, curve)
    ar_second(1)
    energy1, curve1 = ar_third(1)
    mixing = energy1 / energy0
    step1 = energy1 / (curve1 - mixing * energy1 / step0)
    ahead = (step0 + step1 * mixing).reshape(1, 1, N)
    last = step1.reshape(1, 1, N)

    def write(x):
        image[x] = ahead * field[0, x + 1, 1 : B + 1] + last * field[1, x + 1, 1 : B + 1]
        pltpu.make_async_copy(image.at[x], out_hbm.at[x], out_sem.at[x]).start()

    each(0, B, write)
    for copy in unsent:
        copy.wait_send()
    for k in range(2):
        rs_wait(k, True)
        plane_wait(ag, ag_s, ag_r, k, True)
        column_wait(tg, tg_s, tg_r, k, True)
        column_wait(ar1, a1_s, a1_r, k, True)
        plane_wait(ar2, a2_s, a2_r, k, True)
    for copies in [hh] + halos:
        for copy, exists, _, _ in copies:
            pl.when(exists)(copy.wait_send)

    def written(x):
        pltpu.make_async_copy(image.at[x], out_hbm.at[x], out_sem.at[x]).wait()

    each(0, B, written)


def local(
    right_side,
    conductivity,
    reaction,
    leaf_factor,
    leaf_weight,
    leaf_skeleton,
    device_factor,
    device_weight,
    device_skeleton,
    column_factor,
    column_weight,
    column_skeleton,
    top_factor,
):
    leaf_w = jnp.swapaxes(leaf_weight.reshape(8, 512, 64), 1, 2)
    any_space = pl.BlockSpec(memory_space=pl.ANY)
    dma = pltpu.SemaphoreType.DMA
    vm = pltpu.VMEM
    scratch = [
        vm((B, B, B, N), F32),
        vm((B, B, B), F32),
        vm((B, B, B), F32),
        vm((8, 64), jnp.int32),
        vm((1, 256), jnp.int32),
        vm((1, 128), jnp.int32),
        vm((B + 2, B + 2, B, 128), F32),
        vm((B, B, B, 128), F32),
        vm((4, 512, 512), F32),
        vm((8, 512, 512), BF16),
        vm((8, 512, 512), BF16),
        vm((8, 64, 512), F32),
        vm((8, 128, 512), BF16),
        vm((8, 512, 256), BF16),
        vm((512, 512), F32),
        vm((512, 256), F32),
        vm((256, 512), F32),
        vm((256, 2048), F32),
        vm((256, 128), F32),
        vm((128, 256), F32),
        vm((128, 512), F32),
        vm((512, 128), F32),
        vm((128, 2048), F32),
        vm((128, 2048), BF16),
        vm((128, 2048), BF16),
        vm((2, B + 2, B + 2, B, N), F32),
        vm((B, B, B, N), F32),
        vm((512, N), F32),
        vm((512, N), F32),
        vm((2, N, 128), F32),
        vm((2, NS, 256, N), F32),
        vm((256, N), F32),
        vm((2, NS, PIECE, 128), F32),
        vm((2, NPQ, PIECE, 128), F32),
        vm((2, NS, PIECE, 128), F32),
        vm((2, NS, 8, 128), F32),
        vm((2, NPQ, 8, 128), F32),
        vm((2, 2, B, B, N), F32),
        vm((2, 2, B, B, N), F32),
        vm((2, B, B, 128), F32),
        vm((2, B, B, 128), F32),
        dma((21,)),
        dma((B,)),
        dma((2, 14)),
        dma((2, NS, 2)),
        dma((2, NS)),
        dma((2, NS)),
        dma((2, NPQ)),
        dma((2, NPQ)),
        dma((2, NS)),
        dma((2, NS)),
        dma((2, NS)),
        dma((2, NS)),
        dma((2, NPQ)),
        dma((2, NPQ)),
        dma((2, 6)),
        dma((2, 6)),
        dma((6,)),
        dma((6,)),
    ]
    return pl.pallas_call(
        kernel,
        out_shape=jax.ShapeDtypeStruct((B, B, B, N), F32),
        in_specs=[any_space] * 13,
        out_specs=any_space,
        scratch_shapes=scratch,
        compiler_params=pltpu.CompilerParams(
            collective_id=0, has_side_effects=True, vmem_limit_bytes=67043328
        ),
        name="cg",
    )(
        right_side,
        conductivity,
        reaction,
        leaf_factor.reshape(8, 512, 512),
        leaf_w,
        leaf_skeleton.reshape(8, 64),
        device_factor[0, 0, 0],
        device_weight[0, 0, 0],
        device_skeleton.reshape(1, 256),
        column_factor[0, 0],
        column_weight[0, 0],
        column_skeleton.reshape(1, 128),
        top_factor,
    )


def solution(mesh):
    cells = P("gx", "gy", "gz")
    in_specs = (cells,) * 10 + (P("gx", "gy"), P("gx", "gy"), P(("gx", "gy"), None))
    return jax.shard_map(local, mesh=mesh, in_specs=in_specs, out_specs=cells, check_vma=False)
```
